256 devices in a mesh: blk: 64 (over y, z_hi, x), grp: 4 (over z_lo, core).
Axes of the slice: x: 4, y: 4, z: 8 (z_hi: 4, z_lo: 2; z = z_hi * 2 + z_lo), core: 2. Of those that a mesh axis runs over, the one named last changes fastest.
Arguments:
- user_factors: float32 [262144, 128], P(('blk', 'grp')), may hold values from -1.8 to 1.8
- user_accum: float32 [262144], P(('blk', 'grp')), may hold values from 10 to 200
- friend_factors: float32 [262144, 128], P(('blk', 'grp')), may hold values from -1.8 to 1.8
- friend_accum: float32 [262144], P(('blk', 'grp')), may hold values from 10 to 200
- item_factors: float32 [32768, 128], P('blk'), may hold values from -1.8 to 1.8
- item_accum: float32 [32768], P('blk'), may hold values from 10 to 200
- rating_values: bfloat16 [2, 8192, 128, 128], P(None, ('blk', 'grp')), may hold values from -4 to 4
- rating_masks: int32 [2, 8192, 10, 128], P(None, ('blk', 'grp')), may hold values from 0 to 16383, as said below
- rating_rows: int32 [2, 8192], P(None, ('blk', 'grp')), may hold values from 0 to 7, as said below
- rating_cols: int32 [2, 8192], P(None, ('blk', 'grp')), may hold values from 0 to 3, as said below
- rating_counts: int32 [2, 256], P(None, ('blk', 'grp')), may hold values from 1 to 32, as said below
- trust_values: bfloat16 [12288, 128, 128], P(('blk', 'grp')), may hold values from 0 to 1
- trust_masks: int32 [12288, 10, 128], P(('blk', 'grp')), may hold values from 0 to 16383, as said below
- trust_rows: int32 [12288], P(('blk', 'grp')), may hold values from 0 to 7, as said below
- trust_cols: int32 [12288], P(('blk', 'grp')), may hold values from 0 to 7, as said below
- trust_counts: int32 [256], P(('blk', 'grp')), may hold values from 1 to 48, as said below
Outputs:
- user_out: float32 [262144, 128], P(('blk', 'grp'))
- user_acc_out: float32 [262144], P(('blk', 'grp'))
- friend_out: float32 [262144, 128], P(('blk', 'grp'))
- friend_acc_out: float32 [262144], P(('blk', 'grp'))
- item_out: float32 [32768, 128], P(('blk', 'grp'))
- item_acc_out: float32 [32768], P(('blk', 'grp'))
The draws below stay inside these ranges and needn't reach their ends.
Inputs may be any that keep to these rules, and one draw needn't show every extreme that they name: `rating_rows`: in each stratum and group the listed (row, column) tile pairs of all slots are distinct. `rating_cols`: see rating_rows. `rating_counts`: slots at or past the count are ignored; in each stratum some group has all 32 slots live. `rating_masks`: bit i of word w at column c marks row 14 w + i of the tile; bits of rows at or past 128 are zero. `trust_rows`: in each group the listed (row, column) tile pairs of all slots are distinct. `trust_cols`: see trust_rows. `trust_counts`: slots at or past the count are ignored; some group has all 48 slots live. `trust_masks`: bit i of word w at column c marks row 14 w + i of the tile; bits of rows at or past 128 are zero.
All inputs are finite; a program needn't handle non-finite values.
Results may differ from the reference program's by a relative error of at most 0.005.
Values may be sent and summed in bfloat16 or wider, within the bound.
No kernel may reach another device: no remote copies, remote signals or barrier semaphores. Data moves between devices by JAX's collectives and lax.ppermute only.
A program may use at most 64 MiB of HBM per device.

```python
import math
import jax
import jax.numpy as jnp
from jax import lax

FACTOR_RANK = 128
TILE_SIZE = 128
USER_ROWS = 1024
ITEM_ROWS = 512
RATE_SLOTS = 32
SOCIAL_SLOTS = 48
MASK_WORDS = 10
ALL_USERS = 262144
ALL_ITEMS = 32768
N_BLK = 64
N_GRP = 4
DEVICES = 256


def tile_places(key, lanes, slot_total, height, across):
    lane_keys = jax.random.split(key, lanes)

    def choose(lane_key):
        return jax.random.permutation(lane_key, height * across)[:slot_total]
    return jax.vmap(choose)(lane_keys).reshape(-1)


def rating_places(key):
    places = tile_places(jax.random.fold_in(key, 17), 2 * DEVICES, RATE_SLOTS, USER_ROWS // TILE_SIZE, ITEM_ROWS // TILE_SIZE)
    return places.reshape(2, RATE_SLOTS * DEVICES)


def trust_places(key):
    return tile_places(jax.random.fold_in(key, 23), DEVICES, SOCIAL_SLOTS, USER_ROWS // TILE_SIZE, USER_ROWS // TILE_SIZE)


def skewed_counts(key, lines, slot_total):
    key_one, key_two, key_three = jax.random.split(key, 3)
    density = jax.random.randint(key_one, (lines, DEVICES), 0, 4)
    base_count = jnp.maximum(slot_total // jnp.left_shift(1, density), 1)
    jitter = jax.random.randint(key_two, (lines, DEVICES), 0, base_count // 4 + 1)
    counts = jnp.maximum(base_count - jitter, 1)
    chosen = jax.random.randint(key_three, (lines, 1), 0, DEVICES)
    positions = jnp.arange(DEVICES)[None, :]
    return jnp.where(positions == chosen, slot_total, counts).astype(jnp.int32)


def packed_bits(key, leading):
    key_one, key_two, key_three = jax.random.split(key, 3)
    full_shape = leading + (MASK_WORDS, TILE_SIZE)
    top_bits = jax.random.randint(key_one, full_shape, 0, 16384)
    low_bits = jax.random.randint(key_two, full_shape, 0, 16384)
    density = jax.random.randint(key_three, leading + (1, 1), 0, 3)
    packed_words = jnp.where(density == 0, top_bits & low_bits, jnp.where(density == 1, top_bits, top_bits | low_bits))
    kept_rows = TILE_SIZE - 14 * (MASK_WORDS - 1)
    word_limit = jnp.where(jnp.arange(MASK_WORDS) == MASK_WORDS - 1, 2 ** kept_rows - 1, 16383)
    return (packed_words & word_limit[:, None]).astype(jnp.int32)


def draw_rating_rows(key, part):
    return (rating_places(key) // (ITEM_ROWS // TILE_SIZE)).astype(jnp.int32)


def draw_rating_cols(key, part):
    return (rating_places(key) % (ITEM_ROWS // TILE_SIZE)).astype(jnp.int32)


def draw_rating_counts(key, part):
    return skewed_counts(jax.random.fold_in(key, 29), 2, RATE_SLOTS)


def draw_rating_masks(key, part):
    return packed_bits(jax.random.fold_in(key, 41), (2, RATE_SLOTS * DEVICES))


def draw_trust_rows(key, part):
    return (trust_places(key) // (USER_ROWS // TILE_SIZE)).astype(jnp.int32)


def draw_trust_cols(key, part):
    return (trust_places(key) % (USER_ROWS // TILE_SIZE)).astype(jnp.int32)


def draw_trust_counts(key, part):
    return skewed_counts(jax.random.fold_in(key, 31), 1, SOCIAL_SLOTS).reshape(DEVICES)


def draw_trust_masks(key, part):
    return packed_bits(jax.random.fold_in(key, 43), (SOCIAL_SLOTS * DEVICES,))


def block_levels(stream_key, dims, pieces, smallest, high):
    gain = 1.0
    for dim, parts in pieces:
        steps = jax.random.uniform(jax.random.fold_in(jax.random.fold_in(stream_key, 6), dim), (parts,), jnp.float32, smallest / len(pieces), high / len(pieces))
        gain = gain * jnp.repeat(jnp.exp(steps), dims[dim] // parts).reshape((-1,) + (1,) * (len(dims) - 1 - dim))
    return gain


def gaussian(rng, dims, spread, most, shards=(), kind=jnp.bfloat16):
    gain = block_levels(rng, dims, shards, -0.22, 0.18) if shards else 1.0
    values = jax.random.normal(rng, dims, jnp.float32) * spread * gain
    return jnp.minimum(jnp.maximum(values, -most), most).astype(kind)


def setup_inputs(seed: int = 0) -> dict:
    streams_of = jax.random.split(jax.random.key(seed), 17)
    user_factors = gaussian(streams_of[0], (ALL_USERS, FACTOR_RANK), 0.3, 1.8, ((0, 256),), jnp.float32)
    user_accum = jnp.clip(jnp.exp(math.log(200.0) - 2.9957323 * jax.random.uniform(streams_of[1], (ALL_USERS,), jnp.float32) ** block_levels(streams_of[1], (ALL_USERS,), ((0, 256),), -0.2, 0.2)), 10.0, 200.0)
    friend_factors = gaussian(streams_of[2], (ALL_USERS, FACTOR_RANK), 0.3, 1.8, ((0, 256),), jnp.float32)
    friend_accum = jnp.clip(jnp.exp(math.log(200.0) - 2.9957323 * jax.random.uniform(streams_of[3], (ALL_USERS,), jnp.float32) ** block_levels(streams_of[3], (ALL_USERS,), ((0, 256),), -0.2, 0.2)), 10.0, 200.0)
    item_factors = gaussian(streams_of[4], (ALL_ITEMS, FACTOR_RANK), 0.3, 1.8, ((0, 64),), jnp.float32)
    item_accum = jnp.clip(jnp.exp(math.log(200.0) - 2.9957323 * jax.random.uniform(streams_of[5], (ALL_ITEMS,), jnp.float32) ** block_levels(streams_of[5], (ALL_ITEMS,), ((0, 64),), -0.2, 0.2)), 10.0, 200.0)
    rating_values = gaussian(streams_of[6], (2, RATE_SLOTS * DEVICES, TILE_SIZE, TILE_SIZE), 1.0, 4.0, ((1, 256),))
    rating_masks = draw_rating_masks(jax.random.fold_in(streams_of[16], 71), 0)
    rating_rows = draw_rating_rows(jax.random.fold_in(streams_of[16], 71), 0)
    rating_cols = draw_rating_cols(jax.random.fold_in(streams_of[16], 71), 0)
    rating_counts = draw_rating_counts(jax.random.fold_in(streams_of[16], 71), 0)
    trust_values = jnp.clip(1.0 * jax.random.uniform(streams_of[11], (SOCIAL_SLOTS * DEVICES, TILE_SIZE, TILE_SIZE), jnp.float32) ** block_levels(streams_of[11], (SOCIAL_SLOTS * DEVICES, TILE_SIZE, TILE_SIZE), ((0, 256),), -0.2, 0.2), 0.0, 1.0).astype(jnp.bfloat16)
    trust_masks = draw_trust_masks(jax.random.fold_in(streams_of[16], 71), 0)
    trust_rows = draw_trust_rows(jax.random.fold_in(streams_of[16], 71), 0)
    trust_cols = draw_trust_cols(jax.random.fold_in(streams_of[16], 71), 0)
    trust_counts = draw_trust_counts(jax.random.fold_in(streams_of[16], 71), 0)
    return {"user_factors": user_factors, "user_accum": user_accum, "friend_factors": friend_factors, "friend_accum": friend_accum, "item_factors": item_factors, "item_accum": item_accum, "rating_values": rating_values, "rating_masks": rating_masks, "rating_rows": rating_rows, "rating_cols": rating_cols, "rating_counts": rating_counts, "trust_values": trust_values, "trust_masks": trust_masks, "trust_rows": trust_rows, "trust_cols": trust_cols, "trust_counts": trust_counts}


learn_rate = 0.3
shrinkage = 0.02

def unpack_bits(packed_words):
    shifts = jnp.arange(14, dtype=jnp.int32)
    mask_bits = jnp.bitwise_and(jnp.right_shift(packed_words[..., :, None, :], shifts[:, None]), 1)
    mask_bits = mask_bits.reshape(packed_words.shape[:-2] + (packed_words.shape[-2] * 14, packed_words.shape[-1]))
    return mask_bits[..., :TILE_SIZE, :]

def tile_products(left_low, right_low, values, packed_words, tile_rows, tile_cols, live_total):
    slot_total = values.shape[0]
    left_tiles = left_low.reshape(-1, TILE_SIZE, FACTOR_RANK)
    right_tiles = right_low.reshape(-1, TILE_SIZE, FACTOR_RANK)
    left_pick = jnp.take(left_tiles, tile_rows, axis=0).astype(jnp.float32)
    right_pick = jnp.take(right_tiles, tile_cols, axis=0).astype(jnp.float32)
    predict = jnp.einsum('sik,sjk->sij', left_pick, right_pick, precision=lax.Precision.HIGHEST)
    live_slots = (jnp.arange(slot_total, dtype=jnp.int32) < live_total).astype(jnp.float32)
    observed = unpack_bits(packed_words).astype(jnp.float32) * live_slots[:, None, None]
    residual = (observed * (values.astype(jnp.float32) - predict)).astype(jnp.bfloat16)
    residual = lax.optimization_barrier(residual).astype(jnp.float32)
    left_part = jnp.einsum('sij,sjk->sik', residual, right_pick, precision=lax.Precision.HIGHEST)
    right_part = jnp.einsum('sij,sik->sjk', residual, left_pick, precision=lax.Precision.HIGHEST)
    left_sum = jnp.zeros(left_tiles.shape, jnp.float32).at[tile_rows].add(left_part)
    right_sum = jnp.zeros(right_tiles.shape, jnp.float32).at[tile_cols].add(right_part)
    return (left_sum.reshape(-1, FACTOR_RANK), right_sum.reshape(-1, FACTOR_RANK))

def row_update(factor, accum, gradient):
    new_accum = accum + lax.optimization_barrier(jnp.mean(gradient * gradient, axis=-1))
    return (factor - learn_rate * gradient / jnp.sqrt(new_accum)[..., None], new_accum)

def per_device(array):
    return array.reshape((N_BLK, N_GRP, -1) + array.shape[1:])

def rating_stratum(user_state, user_acc, item_state, item_acc, values, packed_words, tile_rows, tile_cols, live_counts, offset):
    user_split = user_state.astype(jnp.bfloat16).reshape(N_BLK, N_GRP, USER_ROWS, FACTOR_RANK)
    item_blocks = jnp.roll(item_state.astype(jnp.bfloat16).reshape(N_BLK, ITEM_ROWS, FACTOR_RANK), offset, axis=0)

    def one_block(packed):
        user_block, item_block, value_block, word_block, row_block, col_block, count_block = packed

        def one_group(user_group, value_group, word_group, row_group, col_group, count_group):
            return tile_products(user_group, item_block, value_group, word_group, row_group, col_group, count_group)
        user_part, item_part = jax.vmap(one_group)(user_block, value_block, word_block, row_block, col_block, count_block)
        return (user_part, lax.optimization_barrier(jnp.sum(item_part, axis=0)))
    user_prod, item_prod = lax.map(one_block, (user_split, item_blocks, per_device(values), per_device(packed_words), per_device(tile_rows), per_device(tile_cols), live_counts.reshape(N_BLK, N_GRP)))
    item_prod = jnp.roll(item_prod, -offset, axis=0).reshape(ALL_ITEMS, FACTOR_RANK)
    user_prod = user_prod.reshape(ALL_USERS, FACTOR_RANK)
    user_state, user_acc = row_update(user_state, user_acc, shrinkage * user_state - user_prod)
    item_state, item_acc = row_update(item_state, item_acc, shrinkage * item_state - item_prod)
    return (user_state, user_acc, item_state, item_acc)

def reference(user_factors, user_accum, friend_factors, friend_accum, item_factors, item_accum, rating_values, rating_masks, rating_rows, rating_cols, rating_counts, trust_values, trust_masks, trust_rows, trust_cols, trust_counts):
    user_state, user_acc, item_state, item_acc = (user_factors, user_accum, item_factors, item_accum)
    for stratum in range(2):
        user_state, user_acc, item_state, item_acc = rating_stratum(user_state, user_acc, item_state, item_acc, rating_values[stratum], rating_masks[stratum], rating_rows[stratum], rating_cols[stratum], rating_counts[stratum], stratum)
    user_split = user_state.astype(jnp.bfloat16).reshape(N_BLK, N_GRP, USER_ROWS, FACTOR_RANK)
    partner = jnp.bitwise_xor(jnp.arange(N_BLK, dtype=jnp.int32), N_BLK // 2)
    friend_split = friend_factors.astype(jnp.bfloat16).reshape(N_BLK, N_GRP, USER_ROWS, FACTOR_RANK)[partner]

    def one_block(packed):
        user_block, friend_block, value_block, word_block, row_block, col_block, count_block = packed
        return jax.vmap(tile_products)(user_block, friend_block, value_block, word_block, row_block, col_block, count_block)
    user_prod, friend_prod = lax.map(one_block, (user_split, friend_split, per_device(trust_values), per_device(trust_masks), per_device(trust_rows), per_device(trust_cols), trust_counts.reshape(N_BLK, N_GRP)))
    friend_prod = friend_prod[partner].reshape(ALL_USERS, FACTOR_RANK)
    user_prod = user_prod.reshape(ALL_USERS, FACTOR_RANK)
    user_out, user_acc_out = row_update(user_state, user_acc, shrinkage * user_state - user_prod)
    friend_out, friend_acc_out = row_update(friend_factors, friend_accum, shrinkage * friend_factors - friend_prod)
    item_out = jnp.roll(item_state.reshape(N_BLK, ITEM_ROWS, FACTOR_RANK), 1, axis=0).reshape(ALL_ITEMS, FACTOR_RANK)
    item_acc_out = jnp.roll(item_acc.reshape(N_BLK, ITEM_ROWS), 1, axis=0).reshape(ALL_ITEMS)
    return (user_out, user_acc_out, friend_out, friend_acc_out, item_out, item_acc_out)
```

```python
import jax
import jax.numpy as jnp
from jax import lax
from jax.experimental import pallas as pl
from jax.experimental.pallas import tpu as pltpu
from jax.sharding import PartitionSpec as P

learn_rate = 0.3
shrinkage = 0.02
T = 128
WORD_BITS = 14
UNSEEN = 2.0**100
SEEN_BELOW = 2.0**90
bf16 = jnp.bfloat16
f32 = jnp.float32
HBM = pl.BlockSpec(memory_space=pl.ANY)
VM = pl.BlockSpec(memory_space=pltpu.VMEM)
SM = pl.BlockSpec(memory_space=pltpu.SMEM)


def shape(dims, dtype):
    return jax.ShapeDtypeStruct(dims, dtype)


def matmul(a, b, ca, cb):
    return lax.dot_general(a, b, (((ca,), (cb,)), ((), ())), preferred_element_type=f32)


def tile(index):
    return slice(index * T, (index + 1) * T)


def call(body, ins, outs, scratch, flops, moved, name):
    return pl.pallas_call(
        body,
        in_specs=ins,
        out_specs=[VM] * len(outs),
        out_shape=outs,
        scratch_shapes=scratch,
        cost_estimate=pl.CostEstimate(flops=flops, bytes_accessed=moved, transcendentals=0),
        name=name,
    )


def bit_patterns():
    rows = lax.broadcasted_iota(jnp.int32, (8, T), 0)
    found = {}
    for k in range(T // 8):
        first = (8 * k) % WORD_BITS
        if first not in found:
            bit = first + rows
            second = bit >= WORD_BITS
            found[first] = (
                jnp.left_shift(1, jnp.where(second, bit - WORD_BITS, bit)),
                second if first > WORD_BITS - 8 else None,
            )
    return found


def observed(patterns, words, slot, k2):
    halves = []
    for k in (2 * k2, 2 * k2 + 1):
        w = 8 * k // WORD_BITS
        bits, second = patterns[8 * k % WORD_BITS]
        word = jnp.broadcast_to(words[w, pl.ds(slot, 1), :], (8, T))
        if second is not None:
            later = jnp.broadcast_to(words[w + 1, pl.ds(slot, 1), :], (8, T))
            word = jnp.where(second, later, word)
        halves.append((word & bits) != 0)
    return jnp.concatenate(halves, axis=0)


def invert_slots(place_of, live, slots, places, spare):
    @pl.loop(0, places)
    def _(t):
        slots[t] = spare

    @pl.loop(0, live)
    def _(q):
        slots[place_of(q)] = q


def column_of(core, j):
    return 2 * (j % 2) + (core if j < 2 else 1 - core)


def zero_spare(words, slot_total):
    words[:, slot_total:, :] = jnp.zeros((words.shape[0], words.shape[1] - slot_total, T), jnp.int32)


def first_stratum(
    rows, cols, counts, user_hbm, item_hbm, acc_hbm, friend_hbm, vals_hbm, masks_hbm,
    own_sum, other_sum, own_resid, other_resid, item_out, friend_low,
    user, item, acc, friend, vals, words, slots, right, sems,
):
    slot_total = vals_hbm.shape[1]
    core = lax.axis_index("grp") % 2
    sources = [
        (vals_hbm.at[0], vals.at[pl.ds(0, slot_total)]),
        (masks_hbm.at[0], words.at[:, pl.ds(0, slot_total), :]),
        (user_hbm, user),
        (item_hbm, item),
        (acc_hbm, acc),
        (friend_hbm, friend),
    ]
    copies = [pltpu.make_async_copy(a, b, sems.at[i]) for i, (a, b) in enumerate(sources)]
    for copy in copies:
        copy.start()
    invert_slots(lambda q: rows[0, q] * 4 + cols[0, q], counts[0, 0], slots, 32, slot_total)
    zero_spare(words, slot_total)
    patterns = bit_patterns()
    copies[3].wait()
    for j in range(4):
        column = column_of(core, j)
        rows_f32 = item[pl.ds(pl.multiple_of(column * T, T), T), :]
        right[tile(j), :] = rows_f32.astype(bf16)
        if j < 2:
            item_out[tile(j), :] = rows_f32
    copies[4].wait()
    item_out[2 * T : 2 * T + 8, :] = jnp.zeros((8, T), f32)
    for j in range(2):
        item_out[2 * T + j : 2 * T + j + 1, :] = acc[pl.ds(column_of(core, j), 1), :]
    for i in (2, 1, 0):
        copies[i].wait()
    user_low = user[...].astype(bf16)
    for r in range(8):
        predict = matmul(user_low[tile(r), :], right[...], 1, 1)
        for j in range(4):
            slot = slots[r * 4 + column_of(core, j)]
            out = own_resid if j < 2 else other_resid
            for k2 in range(T // 16):
                part = slice(16 * k2, 16 * k2 + 16)
                seen = observed(patterns, words, slot, k2)
                diff = vals[slot, part, :].astype(f32) - predict[part, tile(j)]
                out[r * T + 16 * k2 : r * T + 16 * k2 + 16, tile(j % 2)] = jnp.where(seen, diff, 0.0).astype(bf16)
    own_sum[...] = matmul(user_low, own_resid[...], 0, 0)
    other_sum[...] = matmul(user_low, other_resid[...], 0, 0).astype(bf16)
    copies[5].wait()
    friend_low[...] = friend[...].astype(bf16)


def chip_sum(own_sum, arrived, out):
    out[...] = (own_sum[...] + arrived[...].astype(f32)).astype(bf16)


def eye_mask():
    return lax.broadcasted_iota(jnp.int32, (T, T), 0) == lax.broadcasted_iota(jnp.int32, (T, T), 1)


def update_rows(eye, factor, acc_row, prod):
    grad = shrinkage * factor - prod
    spread = jnp.where(eye, jnp.broadcast_to(acc_row, (T, T)), 0.0)
    acc = jnp.sum(grad * grad * (1.0 / T) + spread, axis=1, keepdims=True)
    new = factor - grad * (learn_rate * lax.rsqrt(acc))
    acc_out = jnp.sum(jnp.where(eye, jnp.broadcast_to(acc, (T, T)), 0.0), axis=0, keepdims=True)
    return new, acc_out


def first_users(own_resid, other_resid, user, item, acc, user_mid, acc_mid, user_low):
    core = lax.axis_index("grp") % 2
    eye = eye_mask()
    halves = []
    for first in (0, 2):
        parts = [item[pl.ds(pl.multiple_of(column_of(core, j) * T, T), T), :] for j in (first, first + 1)]
        halves.append(jnp.concatenate(parts, axis=0).astype(bf16))
    prod = matmul(own_resid[...], halves[0], 1, 0) + matmul(other_resid[...], halves[1], 1, 0)
    for r in range(8):
        new, acc_out = update_rows(eye, user[tile(r), :], acc[r : r + 1, :], prod[tile(r), :])
        user_mid[tile(r), :] = new
        user_low[tile(r), :] = new.astype(bf16)
        acc_mid[r : r + 1, :] = acc_out


def place_tiles(
    rows, cols, counts, trust_rows, trust_cols, trust_count, vals_hbm, masks_hbm, trust_hbm, trust_masks_hbm,
    placed, trust_placed, vals, words, trust_vals, trust_words, slots, sems,
):
    core = lax.axis_index("grp") % 2
    rate_total, trust_total = vals_hbm.shape[1], trust_hbm.shape[0]
    sources = [
        (vals_hbm.at[1], vals.at[pl.ds(0, rate_total)]),
        (masks_hbm.at[1], words.at[:, pl.ds(0, rate_total), :]),
        (trust_hbm, trust_vals.at[pl.ds(0, trust_total)]),
        (trust_masks_hbm, trust_words.at[:, pl.ds(0, trust_total), :]),
    ]
    copies = [pltpu.make_async_copy(a, b, sems.at[i]) for i, (a, b) in enumerate(sources)]
    for copy in copies:
        copy.start()
    zero_spare(words, rate_total)
    zero_spare(trust_words, trust_total)
    patterns = bit_patterns()
    invert_slots(lambda q: rows[1, q] * 4 + cols[1, q], counts[1, 0], slots, 32, rate_total)
    copies[0].wait()
    copies[1].wait()

    def place(slot, values, packed, out, r, c):
        for k2 in range(T // 16):
            seen = observed(patterns, packed, slot, k2)
            value = jnp.where(seen, values[slot, 16 * k2 : 16 * k2 + 16, :].astype(f32), UNSEEN)
            out[pl.ds(pl.multiple_of(r * T + 16 * k2, 16), 16), tile(c)] = value.astype(bf16)

    @pl.loop(0, 8)
    def _(r):
        for j in range(4):
            place(slots[r * 4 + column_of(core, j)], vals, words, placed, r, j)

    invert_slots(lambda q: trust_rows[q] * 8 + trust_cols[q], trust_count[0], slots, 64, trust_total)
    copies[2].wait()
    copies[3].wait()

    @pl.loop(0, 8)
    def _(r):
        for c in range(8):
            place(slots[r * 8 + c], trust_vals, trust_words, trust_placed, r, c)


def items_arrive(first, second, item_prev, item_mid, acc_mid, item_low):
    eye = eye_mask()
    total = first[...].astype(f32) + second[...].astype(f32)
    for j in range(2):
        acc_row = item_prev[2 * T + j : 2 * T + j + 1, :]
        new, acc_out = update_rows(eye, item_prev[tile(j), :], acc_row, total[:, tile(j)].T)
        item_mid[tile(j), :] = new
        item_low[tile(j), :] = new.astype(bf16)
        acc_mid[j : j + 1, :] = acc_out


def residuals(left, right, placed, column, out):
    count = right.shape[0] // T
    for r in range(8):
        predict = matmul(left[tile(r), :], right[...], 1, 1)
        for j in range(count):
            value = placed[tile(r), tile(column + j)].astype(f32)
            diff = jnp.where(value < SEEN_BELOW, value - predict[:, tile(j)], 0.0)
            out[tile(r), tile(j)] = diff.astype(bf16)


def own_columns(user_low, own_low, placed, own_resid):
    residuals(user_low, own_low, placed, 0, own_resid)


def second_stratum(
    user_low, own_low, other_low, placed, own_resid, user_mid, acc_mid, far_low, trust_placed,
    other_resid, user_rated, acc_rated, rated_low, trust_resid, friend_sum,
):
    eye = eye_mask()
    residuals(user_low, other_low, placed, 2, other_resid)
    prod = matmul(own_resid[...], own_low[...], 1, 0) + matmul(other_resid[...], other_low[...], 1, 0)
    for r in range(8):
        new, acc_out = update_rows(eye, user_mid[tile(r), :], acc_mid[r : r + 1, :], prod[tile(r), :])
        user_rated[tile(r), :] = new
        rated_low[tile(r), :] = new.astype(bf16)
        acc_rated[r : r + 1, :] = acc_out
    residuals(rated_low, far_low.at[pl.ds(0, 4 * T)], trust_placed, 0, trust_resid)
    friend_sum[...] = matmul(rated_low[...], trust_resid[...], 0, 0).astype(bf16)


def second_half(rated_low, far_low, trust_placed, trust_resid, friend_sum):
    residuals(rated_low, far_low.at[pl.ds(4 * T, 4 * T)], trust_placed, 4, trust_resid)
    friend_sum[...] = matmul(rated_low[...], trust_resid[...], 0, 0).astype(bf16)


def item_products(user_low, own_resid, other_resid, mine, core_part, chip_part, across_part):
    near = lax.axis_index("grp") // 2
    own = matmul(user_low[...], own_resid[...], 0, 0)
    other = matmul(user_low[...], other_resid[...], 0, 0)
    flip = near == 1
    mine[...] = jnp.where(flip, own[:, T:], own[:, :T])
    chip_part[...] = jnp.where(flip, own[:, :T], own[:, T:])
    core_part[...] = jnp.where(flip, other[:, T:], other[:, :T])
    across_part[...] = jnp.where(flip, other[:, :T], other[:, T:])


def last_users(first_resid, second_resid, far_low, user_rated, acc_rated, user_out, acc_out):
    eye = eye_mask()
    half = 4 * T
    prod = matmul(first_resid[...], far_low[:half, :], 1, 0) + matmul(second_resid[...], far_low[half:, :], 1, 0)
    for r in range(8):
        new, acc = update_rows(eye, user_rated[tile(r), :], acc_rated[r : r + 1, :], prod[tile(r), :])
        user_out[tile(r), :] = new
        acc_out[r : r + 1, :] = acc


def last_items(mine, core_part, chip_part, across_part, item_mid, acc_mid, item_out, acc_out):
    near = lax.axis_index("grp") // 2
    total = mine[...] + core_part[...] + chip_part[...] + across_part[...]
    factor = item_mid[pl.ds(pl.multiple_of(near * T, T), T), :]
    new, acc = update_rows(eye_mask(), factor, acc_mid[pl.ds(near, 1), :], total.T)
    item_out[...] = new
    acc_out[...] = acc


def last_friends(first, second, friend, acc, friend_out, acc_out):
    eye = eye_mask()
    for r in range(8):
        arrived = first if r < 4 else second
        prod = arrived[:, tile(r % 4)].astype(f32).T
        new, acc_row = update_rows(eye, friend[tile(r), :], acc[r : r + 1, :], prod)
        friend_out[tile(r), :] = new
        acc_out[r : r + 1, :] = acc_row


def local(
    user_factors, user_accum, friend_factors, friend_accum, item_factors, item_accum,
    rating_values, rating_masks, rating_rows, rating_cols, rating_counts,
    trust_values, trust_masks, trust_rows, trust_cols, trust_counts,
):
    blocks, groups = lax.axis_size("blk"), lax.axis_size("grp")
    axes = ("blk", "grp")

    def send(value, to):
        route = []
        for b in range(blocks):
            for g in range(groups):
                tb, tg = to(b, g)
                route.append((b * groups + g, tb % blocks * groups + tg))
        return lax.ppermute(value, axes, route)

    words_of = rating_masks.transpose(0, 2, 1, 3)
    trust_words_of = trust_masks.transpose(1, 0, 2)
    user_acc = user_accum.reshape(8, T)
    friend_acc = friend_accum.reshape(8, T)
    item_acc = item_accum.reshape(4, T)

    own_sum, other_sum, own_resid, other_resid, item_send, friend_low = call(
        first_stratum,
        [SM, SM, SM] + [HBM] * 6,
        [
            shape((T, 2 * T), f32), shape((T, 2 * T), bf16), shape((8 * T, 2 * T), bf16), shape((8 * T, 2 * T), bf16),
            shape((2 * T + 8, T), f32), shape((8 * T, T), bf16),
        ],
        [
            pltpu.VMEM((8 * T, T), f32), pltpu.VMEM((4 * T, T), f32), pltpu.VMEM((4, T), f32), pltpu.VMEM((8 * T, T), f32),
            pltpu.VMEM((33, T, T), bf16), pltpu.VMEM((10, 40, T), jnp.int32), pltpu.SMEM((32,), jnp.int32),
            pltpu.VMEM((4 * T, T), bf16), pltpu.SemaphoreType.DMA((6,)),
        ],
        270_000_000, 3_000_000, "first_stratum",
    )(rating_rows, rating_cols, rating_counts, user_factors, item_factors, item_acc, friend_factors, rating_values, words_of)

    other_arrived = send(other_sum, lambda b, g: (b, g ^ 1))
    item_prev = send(item_send, lambda b, g: (b + 1, g))
    chip = call(chip_sum, [VM, VM], [shape((T, 2 * T), bf16)], [], 100_000, 300_000, "chip_sum")(own_sum, other_arrived)[0]
    near_sum = send(chip, lambda b, g: (b + 1, g))
    cross_sum = send(chip, lambda b, g: (b + 1, g ^ 2))
    half_bit = blocks // 2
    far_low = send(friend_low, lambda b, g: (b ^ half_bit, g))

    user_mid, acc_mid, user_low = call(
        first_users,
        [VM] * 5,
        [shape((8 * T, T), f32), shape((8, T), f32), shape((8 * T, T), bf16)],
        [], 140_000_000, 3_000_000, "first_users",
    )(own_resid, other_resid, user_factors, item_factors, user_acc)
    placed, trust_placed = call(
        place_tiles,
        [SM] * 6 + [HBM] * 4,
        [shape((8 * T, 4 * T), bf16), shape((8 * T, 8 * T), bf16)],
        [
            pltpu.VMEM((33, T, T), bf16), pltpu.VMEM((10, 40, T), jnp.int32),
            pltpu.VMEM((49, T, T), bf16), pltpu.VMEM((10, 56, T), jnp.int32),
            pltpu.SMEM((64,), jnp.int32), pltpu.SemaphoreType.DMA((4,)),
        ],
        20_000_000, 6_000_000, "place_tiles",
    )(rating_rows, rating_cols, rating_counts, trust_rows, trust_cols, trust_counts, rating_values, words_of, trust_values, trust_words_of)

    item_mid, item_acc_mid, own_low = call(
        items_arrive,
        [VM] * 3,
        [shape((2 * T, T), f32), shape((2, T), f32), shape((2 * T, T), bf16)],
        [], 1_000_000, 500_000, "items_arrive",
    )(near_sum, cross_sum, item_prev)
    other_low = send(own_low, lambda b, g: (b, g ^ 1))
    own_resid = call(
        own_columns, [VM] * 3, [shape((8 * T, 2 * T), bf16)], [], 67_000_000, 1_000_000, "own_columns"
    )(user_low, own_low, placed)[0]
    other_resid, user_rated, acc_rated, rated_low, trust_a, friend_a = call(
        second_stratum,
        [VM] * 9,
        [
            shape((8 * T, 2 * T), bf16), shape((8 * T, T), f32), shape((8, T), f32), shape((8 * T, T), bf16),
            shape((8 * T, 4 * T), bf16), shape((T, 4 * T), bf16),
        ],
        [], 400_000_000, 6_000_000, "second_stratum",
    )(user_low, own_low, other_low, placed, own_resid, user_mid, acc_mid, far_low, trust_placed)
    home_a = send(friend_a, lambda b, g: (b ^ half_bit, g))
    trust_b, friend_b = call(
        second_half,
        [VM] * 3,
        [shape((8 * T, 4 * T), bf16), shape((T, 4 * T), bf16)],
        [], 270_000_000, 3_000_000, "second_half",
    )(rated_low, far_low, trust_placed)
    home_b = send(friend_b, lambda b, g: (b ^ half_bit, g))
    mine, core_part, chip_part, across_part = call(
        item_products,
        [VM] * 3,
        [shape((T, T), f32)] * 4,
        [], 140_000_000, 1_500_000, "item_products",
    )(user_low, own_resid, other_resid)
    core_part = send(core_part, lambda b, g: (b, g ^ 1))
    chip_part = send(chip_part, lambda b, g: (b, g ^ 2))
    across_part = send(across_part, lambda b, g: (b, g ^ 3))
    user_out, user_acc_out = call(
        last_users,
        [VM] * 5,
        [shape((8 * T, T), f32), shape((8, T), f32)],
        [], 270_000_000, 4_000_000, "last_users",
    )(trust_a, trust_b, far_low, user_rated, acc_rated)
    item_out, item_acc_out = call(
        last_items, [VM] * 6, [shape((T, T), f32), shape((1, T), f32)], [], 1_000_000, 400_000, "last_items"
    )(mine, core_part, chip_part, across_part, item_mid, item_acc_mid)
    friend_out, friend_acc_out = call(
        last_friends,
        [VM] * 4,
        [shape((8 * T, T), f32), shape((8, T), f32)],
        [], 4_000_000, 1_500_000, "last_friends",
    )(home_a, home_b, friend_factors, friend_acc)
    return (
        user_out,
        user_acc_out.reshape(8 * T),
        friend_out,
        friend_acc_out.reshape(8 * T),
        item_out,
        item_acc_out.reshape(T),
    )


def solution(mesh):
    both = ("blk", "grp")
    return jax.shard_map(
        local,
        mesh=mesh,
        in_specs=(
            P(both, None), P(both), P(both, None), P(both), P("blk", None), P("blk"),
            P(None, both, None, None), P(None, both, None, None), P(None, both), P(None, both), P(None, both),
            P(both, None, None), P(both, None, None), P(both), P(both), P(both),
        ),
        out_specs=(P(both, None), P(both), P(both, None), P(both), P(both, None), P(both)),
        check_vma=False,
    )
```

```python
import jax
import jax.numpy as jnp
from jax import lax
from jax.experimental import pallas as pl
from jax.experimental.pallas import tpu as pltpu
from jax.sharding import PartitionSpec as P


learn_rate = 0.3
shrinkage = 0.02
T = 128
WORD_BITS = 14
GRANT = 24 * 2**20
UNSEEN = 2.0**100
SEEN_BELOW = 2.0**90
bf16 = jnp.bfloat16
f32 = jnp.float32
HBM = pl.BlockSpec(memory_space=pl.ANY)
SM = pl.BlockSpec(memory_space=pltpu.SMEM)
VM = pl.BlockSpec(memory_space=pltpu.VMEM)


def shape(dims, dtype):
    return jax.ShapeDtypeStruct(dims, dtype)


def matmul(a, b, ca, cb):
    return lax.dot_general(a, b, (((ca,), (cb,)), ((), ())), preferred_element_type=f32)


def tile(index):
    return slice(index * T, (index + 1) * T)


def call(body, ins, outs, scratch, flops, moved):
    inner = pl.pallas_call(
        body,
        in_specs=ins,
        out_specs=[VM] * len(outs),
        out_shape=outs,
        scratch_shapes=scratch,
        cost_estimate=pl.CostEstimate(flops=flops, bytes_accessed=moved, transcendentals=0),
        compiler_params=pltpu.CompilerParams(vmem_limit_bytes=GRANT),
    )

    def run(*args):
        args = [
            pltpu.with_memory_space_constraint(arg, pltpu.HBM) if spec is HBM else arg
            for arg, spec in zip(args, ins, strict=True)
        ]
        return inner(*args)

    return run


def bit_patterns():
    rows = lax.broadcasted_iota(jnp.int32, (8, T), 0)
    found = {}
    for k in range(T // 8):
        first = (8 * k) % WORD_BITS
        if first not in found:
            bit = first + rows
            second = bit >= WORD_BITS
            found[first] = (
                jnp.left_shift(1, jnp.where(second, bit - WORD_BITS, bit)),
                second if first > WORD_BITS - 8 else None,
            )
    return found


def observed(patterns, words, slot, k2):
    halves = []
    for k in (2 * k2, 2 * k2 + 1):
        w = 8 * k // WORD_BITS
        bits, second = patterns[8 * k % WORD_BITS]
        word = jnp.broadcast_to(words[w, pl.ds(slot, 1), :], (8, T))
        if second is not None:
            later = jnp.broadcast_to(words[w + 1, pl.ds(slot, 1), :], (8, T))
            word = jnp.where(second, later, word)
        halves.append((word & bits) != 0)
    return jnp.concatenate(halves, axis=0)


def invert_slots(place_of, live, slots, places, spare):
    @pl.loop(0, places)
    def _(t):
        slots[t] = spare

    @pl.loop(0, live)
    def _(q):
        slots[place_of(q)] = q


def column_of(core, j):
    return 2 * (j % 2) + (core if j < 2 else 1 - core)


def zero_spare(words, slot_total):
    words[:, slot_total:, :] = jnp.zeros((words.shape[0], words.shape[1] - slot_total, T), jnp.int32)


def first_stratum(
    rows_hbm, cols_hbm, counts_hbm, user_hbm, item_hbm, acc_hbm, friend_hbm, vals_hbm, masks_hbm,
    own_sum, other_sum, own_resid, other_resid, item_out, friend_low,
    rows, cols, counts, user, item, acc, friend, vals, words, slots, right, sems,
):
    slot_total = vals_hbm.shape[1]
    core = lax.axis_index("grp") % 2
    sources = [
        (vals_hbm.at[0], vals.at[pl.ds(0, slot_total)]),
        (masks_hbm.at[0], words.at[:, pl.ds(0, slot_total), :]),
        (user_hbm, user),
        (item_hbm, item),
        (acc_hbm, acc),
        (friend_hbm, friend),
        (rows_hbm, rows),
        (cols_hbm, cols),
        (counts_hbm, counts),
    ]
    copies = [pltpu.make_async_copy(a, b, sems.at[i]) for i, (a, b) in enumerate(sources)]
    for i in (6, 7, 8, 0, 1, 3, 4, 2, 5):
        copies[i].start()
    for i in (6, 7, 8):
        copies[i].wait()
    invert_slots(lambda q: rows[0, q] * 4 + cols[0, q], counts[0], slots, 32, slot_total)
    zero_spare(words, slot_total)
    patterns = bit_patterns()
    copies[3].wait()
    for j in range(4):
        column = column_of(core, j)
        rows_f32 = item[pl.ds(pl.multiple_of(column * T, T), T), :]
        right[tile(j), :] = rows_f32.astype(bf16)
        if j < 2:
            item_out[tile(j), :] = rows_f32
    copies[4].wait()
    item_out[2 * T : 2 * T + 8, :] = jnp.zeros((8, T), f32)
    for j in range(2):
        item_out[2 * T + j : 2 * T + j + 1, :] = acc[pl.ds(column_of(core, j), 1), :]
    for i in (2, 1, 0):
        copies[i].wait()
    user_low = user[...].astype(bf16)
    for r in range(8):
        predict = matmul(user_low[tile(r), :], right[...], 1, 1)
        for j in range(4):
            slot = slots[r * 4 + column_of(core, j)]
            out = own_resid if j < 2 else other_resid
            for k2 in range(T // 16):
                part = slice(16 * k2, 16 * k2 + 16)
                seen = observed(patterns, words, slot, k2)
                diff = vals[slot, part, :].astype(f32) - predict[part, tile(j)]
                out[r * T + 16 * k2 : r * T + 16 * k2 + 16, tile(j % 2)] = jnp.where(seen, diff, 0.0).astype(bf16)
    own_sum[...] = matmul(user_low, own_resid[...], 0, 0)
    other_sum[...] = matmul(user_low, other_resid[...], 0, 0).astype(bf16)
    copies[5].wait()
    friend_low[...] = friend[...].astype(bf16)


def chip_sum(own_sum, arrived, out):
    out[...] = (own_sum[...] + arrived[...].astype(f32)).astype(bf16)


def eye_mask():
    return lax.broadcasted_iota(jnp.int32, (T, T), 0) == lax.broadcasted_iota(jnp.int32, (T, T), 1)


def update_rows(eye, factor, acc_row, prod):
    grad = shrinkage * factor - prod
    spread = jnp.where(eye, jnp.broadcast_to(acc_row, (T, T)), 0.0)
    acc = jnp.sum(grad * grad * (1.0 / T) + spread, axis=1, keepdims=True)
    new = factor - grad * (learn_rate * lax.rsqrt(acc))
    acc_out = jnp.sum(jnp.where(eye, jnp.broadcast_to(acc, (T, T)), 0.0), axis=0, keepdims=True)
    return new, acc_out


def first_users(own_resid, other_resid, user, item, acc, user_mid, acc_mid, user_low):
    core = lax.axis_index("grp") % 2
    eye = eye_mask()
    halves = []
    for first in (0, 2):
        parts = [item[pl.ds(pl.multiple_of(column_of(core, j) * T, T), T), :] for j in (first, first + 1)]
        halves.append(jnp.concatenate(parts, axis=0).astype(bf16))
    prod = matmul(own_resid[...], halves[0], 1, 0) + matmul(other_resid[...], halves[1], 1, 0)
    for r in range(8):
        new, acc_out = update_rows(eye, user[tile(r), :], acc[r : r + 1, :], prod[tile(r), :])
        user_mid[tile(r), :] = new
        user_low[tile(r), :] = new.astype(bf16)
        acc_mid[r : r + 1, :] = acc_out


def place_tiles(
    rows_hbm, cols_hbm, counts_hbm, trust_rows_hbm, trust_cols_hbm, trust_count,
    vals_hbm, masks_hbm, trust_hbm, trust_masks_hbm,
    placed, trust_placed, rows, cols, counts, trust_rows, trust_cols, vals, words, trust_vals, trust_words, slots, sems,
):
    core = lax.axis_index("grp") % 2
    rate_total, trust_total = vals_hbm.shape[1], trust_hbm.shape[0]
    sources = [
        (vals_hbm.at[1], vals.at[pl.ds(0, rate_total)]),
        (masks_hbm.at[1], words.at[:, pl.ds(0, rate_total), :]),
        (trust_hbm, trust_vals.at[pl.ds(0, trust_total)]),
        (trust_masks_hbm, trust_words.at[:, pl.ds(0, trust_total), :]),
        (rows_hbm, rows),
        (cols_hbm, cols),
        (counts_hbm, counts),
        (trust_rows_hbm, trust_rows),
        (trust_cols_hbm, trust_cols),
    ]
    copies = [pltpu.make_async_copy(a, b, sems.at[i]) for i, (a, b) in enumerate(sources)]
    for copy in copies[4:] + copies[:4]:
        copy.start()
    for copy in copies[4:]:
        copy.wait()
    zero_spare(words, rate_total)
    zero_spare(trust_words, trust_total)
    patterns = bit_patterns()
    invert_slots(lambda q: rows[1, q] * 4 + cols[1, q], counts[1], slots, 32, rate_total)
    copies[0].wait()
    copies[1].wait()

    def place(slot, values, packed, out, r, c):
        for k2 in range(T // 16):
            seen = observed(patterns, packed, slot, k2)
            value = jnp.where(seen, values[slot, 16 * k2 : 16 * k2 + 16, :].astype(f32), UNSEEN)
            out[pl.ds(pl.multiple_of(r * T + 16 * k2, 16), 16), tile(c)] = value.astype(bf16)

    @pl.loop(0, 8)
    def _(r):
        for j in range(4):
            place(slots[r * 4 + column_of(core, j)], vals, words, placed, r, j)

    invert_slots(lambda q: trust_rows[q] * 8 + trust_cols[q], trust_count[0], slots, 64, trust_total)
    copies[2].wait()
    copies[3].wait()

    @pl.loop(0, 8)
    def _(r):
        for c in range(8):
            place(slots[r * 8 + c], trust_vals, trust_words, trust_placed, r, c)


def items_arrive(first, second, item_prev, item_mid, acc_mid, item_low):
    eye = eye_mask()
    total = first[...].astype(f32) + second[...].astype(f32)
    for j in range(2):
        acc_row = item_prev[2 * T + j : 2 * T + j + 1, :]
        new, acc_out = update_rows(eye, item_prev[tile(j), :], acc_row, total[:, tile(j)].T)
        item_mid[tile(j), :] = new
        item_low[tile(j), :] = new.astype(bf16)
        acc_mid[j : j + 1, :] = acc_out


def residuals(left, right, placed, column, out):
    count = right.shape[0] // T
    for r in range(8):
        predict = matmul(left[tile(r), :], right[...], 1, 1)
        for j in range(count):
            value = placed[tile(r), tile(column + j)].astype(f32)
            diff = jnp.where(value < SEEN_BELOW, value - predict[:, tile(j)], 0.0)
            out[tile(r), tile(j)] = diff.astype(bf16)


def own_columns(user_low, own_low, placed, own_resid):
    residuals(user_low, own_low, placed, 0, own_resid)


def second_stratum(
    user_low, own_low, other_low, placed, own_resid, user_mid, acc_mid, far_low, trust_placed,
    other_resid, user_rated, acc_rated, rated_low, trust_resid, friend_sum,
):
    eye = eye_mask()
    residuals(user_low, other_low, placed, 2, other_resid)
    prod = matmul(own_resid[...], own_low[...], 1, 0) + matmul(other_resid[...], other_low[...], 1, 0)
    for r in range(8):
        new, acc_out = update_rows(eye, user_mid[tile(r), :], acc_mid[r : r + 1, :], prod[tile(r), :])
        user_rated[tile(r), :] = new
        rated_low[tile(r), :] = new.astype(bf16)
        acc_rated[r : r + 1, :] = acc_out
    residuals(rated_low, far_low.at[pl.ds(0, 4 * T)], trust_placed, 0, trust_resid)
    friend_sum[...] = matmul(rated_low[...], trust_resid[...], 0, 0).astype(bf16)


def second_half(rated_low, far_low, trust_placed, trust_resid, friend_sum):
    residuals(rated_low, far_low.at[pl.ds(4 * T, 4 * T)], trust_placed, 4, trust_resid)
    friend_sum[...] = matmul(rated_low[...], trust_resid[...], 0, 0).astype(bf16)


def item_products(user_low, own_resid, other_resid, mine, core_part, chip_part, across_part):
    near = lax.axis_index("grp") // 2
    own = matmul(user_low[...], own_resid[...], 0, 0)
    other = matmul(user_low[...], other_resid[...], 0, 0)
    flip = near == 1
    mine[...] = jnp.where(flip, own[:, T:], own[:, :T])
    chip_part[...] = jnp.where(flip, own[:, :T], own[:, T:])
    core_part[...] = jnp.where(flip, other[:, T:], other[:, :T])
    across_part[...] = jnp.where(flip, other[:, :T], other[:, T:])


def last_users(first_resid, second_resid, far_low, user_rated, acc_rated, user_out, acc_out):
    eye = eye_mask()
    half = 4 * T
    prod = matmul(first_resid[...], far_low[:half, :], 1, 0) + matmul(second_resid[...], far_low[half:, :], 1, 0)
    for r in range(8):
        new, acc = update_rows(eye, user_rated[tile(r), :], acc_rated[r : r + 1, :], prod[tile(r), :])
        user_out[tile(r), :] = new
        acc_out[r : r + 1, :] = acc


def last_items(mine, core_part, chip_part, across_part, item_mid, acc_mid, item_out, acc_out):
    near = lax.axis_index("grp") // 2
    total = mine[...] + core_part[...] + chip_part[...] + across_part[...]
    factor = item_mid[pl.ds(pl.multiple_of(near * T, T), T), :]
    new, acc = update_rows(eye_mask(), factor, acc_mid[pl.ds(near, 1), :], total.T)
    item_out[...] = new
    acc_out[...] = acc


def last_friends(first, second, friend, acc, friend_out, acc_out):
    eye = eye_mask()
    for r in range(8):
        arrived = first if r < 4 else second
        prod = arrived[:, tile(r % 4)].astype(f32).T
        new, acc_row = update_rows(eye, friend[tile(r), :], acc[r : r + 1, :], prod)
        friend_out[tile(r), :] = new
        acc_out[r : r + 1, :] = acc_row


def local(
    user_factors, user_accum, friend_factors, friend_accum, item_factors, item_accum,
    rating_values, rating_masks, rating_rows, rating_cols, rating_counts,
    trust_values, trust_masks, trust_rows, trust_cols, trust_counts,
):
    blocks, groups = lax.axis_size("blk"), lax.axis_size("grp")
    axes = ("blk", "grp")

    def send(value, to):
        route = []
        for b in range(blocks):
            for g in range(groups):
                tb, tg = to(b, g)
                route.append((b * groups + g, tb % blocks * groups + tg))
        return lax.ppermute(value, axes, route)

    words_of = rating_masks.transpose(0, 2, 1, 3)
    trust_words_of = trust_masks.transpose(1, 0, 2)
    user_acc = user_accum.reshape(8, T)
    friend_acc = friend_accum.reshape(8, T)
    item_acc = item_accum.reshape(4, T)
    counts = rating_counts.reshape(2)

    own_sum, other_sum, own_resid, other_resid, item_send, friend_low = call(
        first_stratum,
        [HBM] * 9,
        [
            shape((T, 2 * T), f32), shape((T, 2 * T), bf16), shape((8 * T, 2 * T), bf16), shape((8 * T, 2 * T), bf16),
            shape((2 * T + 8, T), f32), shape((8 * T, T), bf16),
        ],
        [
            pltpu.SMEM((2, 32), jnp.int32), pltpu.SMEM((2, 32), jnp.int32), pltpu.SMEM((2,), jnp.int32),
            pltpu.VMEM((8 * T, T), f32), pltpu.VMEM((4 * T, T), f32), pltpu.VMEM((4, T), f32), pltpu.VMEM((8 * T, T), f32),
            pltpu.VMEM((33, T, T), bf16), pltpu.VMEM((10, 40, T), jnp.int32), pltpu.SMEM((32,), jnp.int32),
            pltpu.VMEM((4 * T, T), bf16), pltpu.SemaphoreType.DMA((9,)),
        ],
        270_000_000, 3_000_000,
    )(rating_rows, rating_cols, counts, user_factors, item_factors, item_acc, friend_factors, rating_values, words_of)

    other_arrived = send(other_sum, lambda b, g: (b, g ^ 1))
    item_prev = send(item_send, lambda b, g: (b + 1, g))
    chip = call(chip_sum, [VM, VM], [shape((T, 2 * T), bf16)], [], 100_000, 300_000)(own_sum, other_arrived)[0]
    near_sum = send(chip, lambda b, g: (b + 1, g))
    cross_sum = send(chip, lambda b, g: (b + 1, g ^ 2))
    half_bit = blocks // 2
    far_low = send(friend_low, lambda b, g: (b ^ half_bit, g))

    user_mid, acc_mid, user_low = call(
        first_users,
        [VM] * 5,
        [shape((8 * T, T), f32), shape((8, T), f32), shape((8 * T, T), bf16)],
        [], 140_000_000, 3_000_000,
    )(own_resid, other_resid, user_factors, item_factors, user_acc)
    placed, trust_placed = call(
        place_tiles,
        [HBM] * 5 + [SM] + [HBM] * 4,
        [shape((8 * T, 4 * T), bf16), shape((8 * T, 8 * T), bf16)],
        [
            pltpu.SMEM((2, 32), jnp.int32), pltpu.SMEM((2, 32), jnp.int32), pltpu.SMEM((2,), jnp.int32),
            pltpu.SMEM((48,), jnp.int32), pltpu.SMEM((48,), jnp.int32),
            pltpu.VMEM((33, T, T), bf16), pltpu.VMEM((10, 40, T), jnp.int32),
            pltpu.VMEM((49, T, T), bf16), pltpu.VMEM((10, 56, T), jnp.int32),
            pltpu.SMEM((64,), jnp.int32), pltpu.SemaphoreType.DMA((9,)),
        ],
        20_000_000, 6_000_000,
    )(rating_rows, rating_cols, counts, trust_rows, trust_cols, trust_counts, rating_values, words_of, trust_values, trust_words_of)

    item_mid, item_acc_mid, own_low = call(
        items_arrive,
        [VM] * 3,
        [shape((2 * T, T), f32), shape((2, T), f32), shape((2 * T, T), bf16)],
        [], 1_000_000, 500_000,
    )(near_sum, cross_sum, item_prev)
    other_low = send(own_low, lambda b, g: (b, g ^ 1))
    own_resid = call(
        own_columns, [VM] * 3, [shape((8 * T, 2 * T), bf16)], [], 67_000_000, 1_000_000
    )(user_low, own_low, placed)[0]
    other_resid, user_rated, acc_rated, rated_low, trust_a, friend_a = call(
        second_stratum,
        [VM] * 9,
        [
            shape((8 * T, 2 * T), bf16), shape((8 * T, T), f32), shape((8, T), f32), shape((8 * T, T), bf16),
            shape((8 * T, 4 * T), bf16), shape((T, 4 * T), bf16),
        ],
        [], 400_000_000, 6_000_000,
    )(user_low, own_low, other_low, placed, own_resid, user_mid, acc_mid, far_low, trust_placed)
    home_a = send(friend_a, lambda b, g: (b ^ half_bit, g))
    trust_b, friend_b = call(
        second_half,
        [VM] * 3,
        [shape((8 * T, 4 * T), bf16), shape((T, 4 * T), bf16)],
        [], 270_000_000, 3_000_000,
    )(rated_low, far_low, trust_placed)
    home_b = send(friend_b, lambda b, g: (b ^ half_bit, g))
    mine, core_part, chip_part, across_part = call(
        item_products,
        [VM] * 3,
        [shape((T, T), f32)] * 4,
        [], 140_000_000, 1_500_000,
    )(user_low, own_resid, other_resid)
    core_part = send(core_part, lambda b, g: (b, g ^ 1))
    chip_part = send(chip_part, lambda b, g: (b, g ^ 2))
    across_part = send(across_part, lambda b, g: (b, g ^ 3))
    user_out, user_acc_out = call(
        last_users,
        [VM] * 5,
        [shape((8 * T, T), f32), shape((8, T), f32)],
        [], 270_000_000, 4_000_000,
    )(trust_a, trust_b, far_low, user_rated, acc_rated)
    item_out, item_acc_out = call(
        last_items, [VM] * 6, [shape((T, T), f32), shape((1, T), f32)], [], 1_000_000, 400_000
    )(mine, core_part, chip_part, across_part, item_mid, item_acc_mid)
    friend_out, friend_acc_out = call(
        last_friends,
        [VM] * 4,
        [shape((8 * T, T), f32), shape((8, T), f32)],
        [], 4_000_000, 1_500_000,
    )(home_a, home_b, friend_factors, friend_acc)
    return (
        user_out,
        user_acc_out.reshape(8 * T),
        friend_out,
        friend_acc_out.reshape(8 * T),
        item_out,
        item_acc_out.reshape(T),
    )


def solution(mesh):
    both = ("blk", "grp")
    return jax.shard_map(
        local,
        mesh=mesh,
        in_specs=(
            P(both, None), P(both), P(both, None), P(both), P("blk", None), P("blk"),
            P(None, both, None, None), P(None, both, None, None), P(None, both), P(None, both), P(None, both),
            P(both, None, None), P(both, None, None), P(both), P(both), P(both),
        ),
        out_specs=(P(both, None), P(both), P(both, None), P(both), P(both, None), P(both)),
        check_vma=False,
    )
```

```python
import jax
import jax.numpy as jnp
from jax import lax
from jax.experimental import pallas as pl
from jax.experimental.pallas import tpu as pltpu
from jax.sharding import PartitionSpec as P


learn_rate = 0.3
shrinkage = 0.02
T = 128
WORD_BITS = 14
GRANT = 24 * 2**20
UNSEEN = 2.0**100
SEEN_BELOW = 2.0**90
bf16 = jnp.bfloat16
f32 = jnp.float32
HBM = pl.BlockSpec(memory_space=pl.ANY)
SM = pl.BlockSpec(memory_space=pltpu.SMEM)
VM = pl.BlockSpec(memory_space=pltpu.VMEM)


def shape(dims, dtype):
    return jax.ShapeDtypeStruct(dims, dtype)


def matmul(a, b, ca, cb):
    return lax.dot_general(a, b, (((ca,), (cb,)), ((), ())), preferred_element_type=f32)


def tile(index):
    return slice(index * T, (index + 1) * T)


def call(body, ins, outs, scratch, flops, moved):
    inner = pl.pallas_call(
        body,
        in_specs=ins,
        out_specs=[VM] * len(outs),
        out_shape=outs,
        scratch_shapes=scratch,
        cost_estimate=pl.CostEstimate(flops=flops, bytes_accessed=moved, transcendentals=0),
        compiler_params=pltpu.CompilerParams(vmem_limit_bytes=GRANT),
    )

    def run(*args):
        args = [
            pltpu.with_memory_space_constraint(arg, pltpu.HBM) if spec is HBM else arg
            for arg, spec in zip(args, ins, strict=True)
        ]
        return inner(*args)

    return run


def bit_patterns():
    rows = lax.broadcasted_iota(jnp.int32, (8, T), 0)
    found = {}
    for k in range(T // 8):
        first = (8 * k) % WORD_BITS
        if first not in found:
            bit = first + rows
            second = bit >= WORD_BITS
            found[first] = (
                jnp.left_shift(1, jnp.where(second, bit - WORD_BITS, bit)),
                second if first > WORD_BITS - 8 else None,
            )
    return found


def observed(patterns, words, slot, k2):
    halves = []
    for k in (2 * k2, 2 * k2 + 1):
        w = 8 * k // WORD_BITS
        bits, second = patterns[8 * k % WORD_BITS]
        word = jnp.broadcast_to(words[w, pl.ds(slot, 1), :], (8, T))
        if second is not None:
            later = jnp.broadcast_to(words[w + 1, pl.ds(slot, 1), :], (8, T))
            word = jnp.where(second, later, word)
        halves.append((word & bits) != 0)
    return jnp.concatenate(halves, axis=0)


def invert_slots(place_of, live, slots, places, spare, total):
    for t in range(places):
        slots[t] = spare
    for q in range(total):
        slots[jnp.where(q < live, place_of(q), places)] = q


def column_of(core, j):
    return 2 * (j % 2) + (core if j < 2 else 1 - core)


def zero_spare(words, slot_total):
    words[:, slot_total:, :] = jnp.zeros((words.shape[0], words.shape[1] - slot_total, T), jnp.int32)


def first_stratum(
    rows_hbm, cols_hbm, counts_hbm, user_hbm, item_hbm, vals_hbm, masks_hbm,
    own_sum, other_sum, own_resid, other_resid,
    rows, cols, counts, user, item, vals, words, slots, right, sems,
):
    slot_total = vals_hbm.shape[1]
    core = lax.axis_index("grp") % 2
    sources = [
        (rows_hbm, rows),
        (cols_hbm, cols),
        (counts_hbm, counts),
        (vals_hbm.at[0], vals.at[pl.ds(0, slot_total)]),
        (masks_hbm.at[0], words.at[:, pl.ds(0, slot_total), :]),
        (item_hbm, item),
        (user_hbm, user),
    ]
    copies = [pltpu.make_async_copy(a, b, sems.at[i]) for i, (a, b) in enumerate(sources)]
    for copy in copies:
        copy.start()
    for copy in copies[:3]:
        copy.wait()
    invert_slots(lambda q: rows[0, q] * 4 + cols[0, q], counts[0], slots, 32, slot_total, slot_total)
    zero_spare(words, slot_total)
    patterns = bit_patterns()
    copies[5].wait()
    for j in range(4):
        right[tile(j), :] = item[pl.ds(pl.multiple_of(column_of(core, j) * T, T), T), :].astype(bf16)
    for i in (6, 4, 3):
        copies[i].wait()
    user_low = user[...].astype(bf16)
    for r in range(8):
        predict = matmul(user_low[tile(r), :], right[...], 1, 1)
        for j in range(4):
            slot = slots[r * 4 + column_of(core, j)]
            out = own_resid if j < 2 else other_resid
            for k2 in range(T // 16):
                part = slice(16 * k2, 16 * k2 + 16)
                seen = observed(patterns, words, slot, k2)
                diff = vals[slot, part, :].astype(f32) - predict[part, tile(j)]
                out[r * T + 16 * k2 : r * T + 16 * k2 + 16, tile(j % 2)] = jnp.where(seen, diff, 0.0).astype(bf16)
    own_sum[...] = matmul(user_low, own_resid[...], 0, 0)
    other_sum[...] = matmul(user_low, other_resid[...], 0, 0)


def chip_sum(own_sum, arrived, kept, sent):
    total = own_sum[...] + arrived[...]
    kept[...] = total
    sent[...] = total.astype(bf16)


def cast_friends(friend, friend_low):
    friend_low[...] = friend[...].astype(bf16)


def eye_mask():
    return lax.broadcasted_iota(jnp.int32, (T, T), 0) == lax.broadcasted_iota(jnp.int32, (T, T), 1)


def update_rows(eye, factor, acc_row, prod):
    grad = shrinkage * factor - prod
    spread = jnp.where(eye, jnp.broadcast_to(acc_row, (T, T)), 0.0)
    acc = jnp.sum(grad * grad * (1.0 / T) + spread, axis=1, keepdims=True)
    new = factor - grad * (learn_rate * lax.rsqrt(acc))
    acc_out = jnp.sum(jnp.where(eye, jnp.broadcast_to(acc, (T, T)), 0.0), axis=0, keepdims=True)
    return new, acc_out


def first_users(own_resid, other_resid, user, item, acc, user_mid, acc_mid, user_low):
    core = lax.axis_index("grp") % 2
    eye = eye_mask()
    halves = []
    for first in (0, 2):
        parts = [item[pl.ds(pl.multiple_of(column_of(core, j) * T, T), T), :] for j in (first, first + 1)]
        halves.append(jnp.concatenate(parts, axis=0).astype(bf16))
    prod = matmul(own_resid[...], halves[0], 1, 0) + matmul(other_resid[...], halves[1], 1, 0)
    for r in range(8):
        new, acc_out = update_rows(eye, user[tile(r), :], acc[r : r + 1, :], prod[tile(r), :])
        user_mid[tile(r), :] = new
        user_low[tile(r), :] = new.astype(bf16)
        acc_mid[r : r + 1, :] = acc_out


def place_tiles(
    rows_hbm, cols_hbm, counts_hbm, trust_rows_hbm, trust_cols_hbm, trust_count,
    vals_hbm, masks_hbm, trust_hbm, trust_masks_hbm,
    placed, trust_placed, rows, cols, counts, trust_rows, trust_cols, vals, words, trust_vals, trust_words, slots, sems,
):
    core = lax.axis_index("grp") % 2
    rate_total, trust_total = vals_hbm.shape[1], trust_hbm.shape[0]
    sources = [
        (vals_hbm.at[1], vals.at[pl.ds(0, rate_total)]),
        (masks_hbm.at[1], words.at[:, pl.ds(0, rate_total), :]),
        (trust_hbm, trust_vals.at[pl.ds(0, trust_total)]),
        (trust_masks_hbm, trust_words.at[:, pl.ds(0, trust_total), :]),
        (rows_hbm, rows),
        (cols_hbm, cols),
        (counts_hbm, counts),
        (trust_rows_hbm, trust_rows),
        (trust_cols_hbm, trust_cols),
    ]
    copies = [pltpu.make_async_copy(a, b, sems.at[i]) for i, (a, b) in enumerate(sources)]
    for copy in copies[4:] + copies[:4]:
        copy.start()
    for copy in copies[4:]:
        copy.wait()
    zero_spare(words, rate_total)
    zero_spare(trust_words, trust_total)
    patterns = bit_patterns()
    invert_slots(lambda q: rows[1, q] * 4 + cols[1, q], counts[1], slots, 32, rate_total, rate_total)
    copies[0].wait()
    copies[1].wait()

    def place(slot, values, packed, out, r, c):
        for k2 in range(T // 16):
            seen = observed(patterns, packed, slot, k2)
            value = jnp.where(seen, values[slot, 16 * k2 : 16 * k2 + 16, :].astype(f32), UNSEEN)
            out[pl.ds(pl.multiple_of(r * T + 16 * k2, 16), 16), tile(c)] = value.astype(bf16)

    @pl.loop(0, 8)
    def _(r):
        for j in range(4):
            place(slots[r * 4 + column_of(core, j)], vals, words, placed, r, j)

    invert_slots(lambda q: trust_rows[q] * 8 + trust_cols[q], trust_count[0], slots, 64, trust_total, trust_total)
    copies[2].wait()
    copies[3].wait()

    @pl.loop(0, 8)
    def _(r):
        for c in range(8):
            place(slots[r * 8 + c], trust_vals, trust_words, trust_placed, r, c)


def update_items(kept, arrived, item, acc, share, item_low):
    core = lax.axis_index("grp") % 2
    near = lax.axis_index("grp") // 2
    eye = eye_mask()
    total = kept[...] + arrived[...].astype(f32)
    share[T : T + 8, :] = jnp.zeros((8, T), f32)
    for j in range(2):
        column = column_of(core, j)
        factor = item[pl.ds(pl.multiple_of(column * T, T), T), :]
        new, acc_out = update_rows(eye, factor, acc[pl.ds(column, 1), :], total[:, tile(j)].T)
        item_low[tile(j), :] = new.astype(bf16)

        @pl.when(near == j)
        def _():
            share[:T, :] = new
            share[T : T + 1, :] = acc_out


def residuals(left, right, placed, column, out):
    count = right.shape[0] // T
    for r in range(8):
        predict = matmul(left[tile(r), :], right[...], 1, 1)
        for j in range(count):
            value = placed[tile(r), tile(column + j)].astype(f32)
            diff = jnp.where(value < SEEN_BELOW, value - predict[:, tile(j)], 0.0)
            out[tile(r), tile(j)] = diff.astype(bf16)


def own_columns(user_low, own_low, placed, own_resid, own_sum):
    residuals(user_low, own_low, placed, 0, own_resid)
    own_sum[...] = matmul(user_low[...], own_resid[...], 0, 0)


def second_stratum(
    user_low, own_low, other_low, placed, own_resid, user_mid, acc_mid, far_low, trust_placed,
    other_resid, user_rated, acc_rated, rated_low, trust_resid, friend_sum,
):
    eye = eye_mask()
    residuals(user_low, other_low, placed, 2, other_resid)
    prod = matmul(own_resid[...], own_low[...], 1, 0) + matmul(other_resid[...], other_low[...], 1, 0)
    for r in range(8):
        new, acc_out = update_rows(eye, user_mid[tile(r), :], acc_mid[r : r + 1, :], prod[tile(r), :])
        user_rated[tile(r), :] = new
        rated_low[tile(r), :] = new.astype(bf16)
        acc_rated[r : r + 1, :] = acc_out
    residuals(rated_low, far_low.at[pl.ds(0, 4 * T)], trust_placed, 0, trust_resid)
    friend_sum[...] = matmul(rated_low[...], trust_resid[...], 0, 0).astype(bf16)


def second_half(rated_low, far_low, trust_placed, trust_resid, friend_sum):
    residuals(rated_low, far_low.at[pl.ds(4 * T, 4 * T)], trust_placed, 4, trust_resid)
    friend_sum[...] = matmul(rated_low[...], trust_resid[...], 0, 0).astype(bf16)


def item_products(user_low, other_resid, other_sum):
    other_sum[...] = matmul(user_low[...], other_resid[...], 0, 0)


def split_sum(own_sum, arrived, kept, sent):
    flip = lax.axis_index("grp") // 2 == 1
    total = own_sum[...] + arrived[...]
    kept[...] = jnp.where(flip, total[:, T:], total[:, :T])
    sent[...] = jnp.where(flip, total[:, :T], total[:, T:])


def last_users(first_resid, second_resid, far_low, user_rated, acc_rated, user_out, acc_out):
    eye = eye_mask()
    half = 4 * T
    prod = matmul(first_resid[...], far_low[:half, :], 1, 0) + matmul(second_resid[...], far_low[half:, :], 1, 0)
    for r in range(8):
        new, acc = update_rows(eye, user_rated[tile(r), :], acc_rated[r : r + 1, :], prod[tile(r), :])
        user_out[tile(r), :] = new
        acc_out[r : r + 1, :] = acc


def last_items(kept, arrived, share, item_out, acc_out):
    new, acc = update_rows(eye_mask(), share[:T, :], share[T : T + 1, :], (kept[...] + arrived[...]).T)
    item_out[...] = new
    acc_out[...] = acc


def last_friends(first, second, friend, acc, friend_out, acc_out):
    eye = eye_mask()
    for r in range(8):
        arrived = first if r < 4 else second
        prod = arrived[:, tile(r % 4)].astype(f32).T
        new, acc_row = update_rows(eye, friend[tile(r), :], acc[r : r + 1, :], prod)
        friend_out[tile(r), :] = new
        acc_out[r : r + 1, :] = acc_row


def local(
    user_factors, user_accum, friend_factors, friend_accum, item_factors, item_accum,
    rating_values, rating_masks, rating_rows, rating_cols, rating_counts,
    trust_values, trust_masks, trust_rows, trust_cols, trust_counts,
):
    blocks, groups = lax.axis_size("blk"), lax.axis_size("grp")
    axes = ("blk", "grp")

    def send(value, to):
        route = []
        for b in range(blocks):
            for g in range(groups):
                tb, tg = to(b, g)
                route.append((b * groups + g, tb % blocks * groups + tg))
        return lax.ppermute(value, axes, route)

    words_of = rating_masks.transpose(0, 2, 1, 3)
    trust_words_of = trust_masks.transpose(1, 0, 2)
    user_acc = user_accum.reshape(8, T)
    friend_acc = friend_accum.reshape(8, T)
    item_acc = item_accum.reshape(4, T)
    counts = rating_counts.reshape(2)

    own_sum, other_sum, own_resid, other_resid = call(
        first_stratum,
        [HBM] * 7,
        [shape((T, 2 * T), f32), shape((T, 2 * T), f32), shape((8 * T, 2 * T), bf16), shape((8 * T, 2 * T), bf16)],
        [
            pltpu.SMEM((2, 32), jnp.int32), pltpu.SMEM((2, 32), jnp.int32), pltpu.SMEM((2,), jnp.int32),
            pltpu.VMEM((8 * T, T), f32), pltpu.VMEM((4 * T, T), f32),
            pltpu.VMEM((33, T, T), bf16), pltpu.VMEM((10, 40, T), jnp.int32), pltpu.SMEM((40,), jnp.int32),
            pltpu.VMEM((4 * T, T), bf16), pltpu.SemaphoreType.DMA((7,)),
        ],
        270_000_000, 3_000_000,
    )(rating_rows, rating_cols, counts, user_factors, item_factors, rating_values, words_of)

    arrived = send(other_sum, lambda b, g: (b, g ^ 1))
    half_bit = blocks // 2
    friend_low = call(cast_friends, [VM], [shape((8 * T, T), bf16)], [], 100_000, 800_000)(friend_factors)[0]
    far_low = send(friend_low, lambda b, g: (b ^ half_bit, g))
    kept, sent = call(
        chip_sum, [VM, VM], [shape((T, 2 * T), f32), shape((T, 2 * T), bf16)], [], 100_000, 300_000
    )(own_sum, arrived)
    arrived = send(sent, lambda b, g: (b, g ^ 2))
    share, own_low = call(
        update_items,
        [VM] * 4,
        [shape((T + 8, T), f32), shape((2 * T, T), bf16)],
        [], 1_000_000, 500_000,
    )(kept, arrived, item_factors, item_acc)
    own_low = send(own_low, lambda b, g: (b + 1, g))
    share = send(share, lambda b, g: (b + 1, g))
    user_mid, acc_mid, user_low = call(
        first_users,
        [VM] * 5,
        [shape((8 * T, T), f32), shape((8, T), f32), shape((8 * T, T), bf16)],
        [], 140_000_000, 3_000_000,
    )(own_resid, other_resid, user_factors, item_factors, user_acc)
    placed, trust_placed = call(
        place_tiles,
        [HBM] * 5 + [SM] + [HBM] * 4,
        [shape((8 * T, 4 * T), bf16), shape((8 * T, 8 * T), bf16)],
        [
            pltpu.SMEM((2, 32), jnp.int32), pltpu.SMEM((2, 32), jnp.int32), pltpu.SMEM((2,), jnp.int32),
            pltpu.SMEM((48,), jnp.int32), pltpu.SMEM((48,), jnp.int32),
            pltpu.VMEM((33, T, T), bf16), pltpu.VMEM((10, 40, T), jnp.int32),
            pltpu.VMEM((49, T, T), bf16), pltpu.VMEM((10, 56, T), jnp.int32),
            pltpu.SMEM((72,), jnp.int32), pltpu.SemaphoreType.DMA((9,)),
        ],
        20_000_000, 6_000_000,
    )(rating_rows, rating_cols, counts, trust_rows, trust_cols, trust_counts, rating_values, words_of, trust_values, trust_words_of)

    other_low = send(own_low, lambda b, g: (b, g ^ 1))
    own_resid, own_sum = call(
        own_columns,
        [VM] * 3,
        [shape((8 * T, 2 * T), bf16), shape((T, 2 * T), f32)],
        [], 140_000_000, 1_000_000,
    )(user_low, own_low, placed)
    other_resid, user_rated, acc_rated, rated_low, trust_a, friend_a = call(
        second_stratum,
        [VM] * 9,
        [
            shape((8 * T, 2 * T), bf16), shape((8 * T, T), f32), shape((8, T), f32), shape((8 * T, T), bf16),
            shape((8 * T, 4 * T), bf16), shape((T, 4 * T), bf16),
        ],
        [], 400_000_000, 6_000_000,
    )(user_low, own_low, other_low, placed, own_resid, user_mid, acc_mid, far_low, trust_placed)
    home_a = send(friend_a, lambda b, g: (b ^ half_bit, g))
    trust_b, friend_b = call(
        second_half,
        [VM] * 3,
        [shape((8 * T, 4 * T), bf16), shape((T, 4 * T), bf16)],
        [], 270_000_000, 3_000_000,
    )(rated_low, far_low, trust_placed)
    home_b = send(friend_b, lambda b, g: (b ^ half_bit, g))
    other_sum = call(
        item_products, [VM] * 2, [shape((T, 2 * T), f32)], [], 70_000_000, 900_000
    )(user_low, other_resid)[0]
    arrived = send(other_sum, lambda b, g: (b, g ^ 1))
    user_out, user_acc_out = call(
        last_users,
        [VM] * 5,
        [shape((8 * T, T), f32), shape((8, T), f32)],
        [], 270_000_000, 4_000_000,
    )(trust_a, trust_b, far_low, user_rated, acc_rated)
    kept, sent = call(split_sum, [VM, VM], [shape((T, T), f32)] * 2, [], 100_000, 400_000)(own_sum, arrived)
    arrived = send(sent, lambda b, g: (b, g ^ 2))
    item_out, item_acc_out = call(
        last_items, [VM] * 3, [shape((T, T), f32), shape((1, T), f32)], [], 1_000_000, 400_000
    )(kept, arrived, share)
    friend_out, friend_acc_out = call(
        last_friends, [VM] * 4, [shape((8 * T, T), f32), shape((8, T), f32)], [], 4_000_000, 1_500_000
    )(home_a, home_b, friend_factors, friend_acc)
    return (
        user_out,
        user_acc_out.reshape(8 * T),
        friend_out,
        friend_acc_out.reshape(8 * T),
        item_out,
        item_acc_out.reshape(T),
    )


def solution(mesh):
    both = ("blk", "grp")
    return jax.shard_map(
        local,
        mesh=mesh,
        in_specs=(
            P(both, None), P(both), P(both, None), P(both), P("blk", None), P("blk"),
            P(None, both, None, None), P(None, both, None, None), P(None, both), P(None, both), P(None, both),
            P(both, None, None), P(both, None, None), P(both), P(both), P(both),
        ),
        out_specs=(P(both, None), P(both), P(both, None), P(both), P(both, None), P(both)),
        check_vma=False,
    )
```

```python
import jax
import jax.numpy as jnp
from jax import lax
from jax.experimental import pallas as pl
from jax.experimental.pallas import tpu as pltpu
from jax.sharding import PartitionSpec as P


learn_rate = 0.3
shrinkage = 0.02
T = 128
WORD_BITS = 14
GRANT = 24 * 2**20
UNSEEN = 2.0**100
SEEN_BELOW = 2.0**90
bf16 = jnp.bfloat16
f32 = jnp.float32
HBM = pl.BlockSpec(memory_space=pl.ANY)
SM = pl.BlockSpec(memory_space=pltpu.SMEM)
VM = pl.BlockSpec(memory_space=pltpu.VMEM)


def shape(dims, dtype):
    return jax.ShapeDtypeStruct(dims, dtype)


def matmul(a, b, ca, cb):
    return lax.dot_general(a, b, (((ca,), (cb,)), ((), ())), preferred_element_type=f32)


def tile(index):
    return slice(index * T, (index + 1) * T)


def call(body, ins, outs, scratch, flops, moved, out_specs=None, aliases=None):
    inner = pl.pallas_call(
        body,
        in_specs=ins,
        out_specs=out_specs or [VM] * len(outs),
        out_shape=outs,
        scratch_shapes=scratch,
        input_output_aliases=aliases or {},
        cost_estimate=pl.CostEstimate(flops=flops, bytes_accessed=moved, transcendentals=0),
        compiler_params=pltpu.CompilerParams(vmem_limit_bytes=GRANT),
    )

    def run(*args):
        args = [
            pltpu.with_memory_space_constraint(arg, pltpu.HBM) if spec is HBM else arg
            for arg, spec in zip(args, ins, strict=True)
        ]
        return inner(*args)

    return run


def bit_patterns():
    rows = lax.broadcasted_iota(jnp.int32, (8, T), 0)
    found = {}
    for k in range(T // 8):
        first = (8 * k) % WORD_BITS
        if first not in found:
            bit = first + rows
            second = bit >= WORD_BITS
            found[first] = (
                jnp.left_shift(1, jnp.where(second, bit - WORD_BITS, bit)),
                second if first > WORD_BITS - 8 else None,
            )
    return found


def observed(patterns, words, slot, k2):
    halves = []
    for k in (2 * k2, 2 * k2 + 1):
        w = 8 * k // WORD_BITS
        bits, second = patterns[8 * k % WORD_BITS]
        word = jnp.broadcast_to(words[w, pl.ds(slot, 1), :], (8, T))
        if second is not None:
            later = jnp.broadcast_to(words[w + 1, pl.ds(slot, 1), :], (8, T))
            word = jnp.where(second, later, word)
        halves.append((word & bits) != 0)
    return jnp.concatenate(halves, axis=0)


def invert_slots(place_of, live, slots, places, spare, total):
    for t in range(places):
        slots[t] = spare
    for q in range(total):
        slots[jnp.where(q < live, place_of(q), places)] = q


def column_of(core, j):
    return 2 * (j % 2) + (core if j < 2 else 1 - core)


def zero_spare(words, slot_total):
    words[:, slot_total:, :] = jnp.zeros((words.shape[0], words.shape[1] - slot_total, T), jnp.int32)


def first_stratum(
    rows_hbm, cols_hbm, counts_hbm, user_hbm, item_hbm, vals_hbm, masks_hbm,
    own_sum, other_sum, own_resid, other_resid,
    rows, cols, counts, user, item, vals, words, slots, right, sems,
):
    slot_total = vals_hbm.shape[1]
    core = lax.axis_index("grp") % 2
    sources = [
        (rows_hbm, rows),
        (cols_hbm, cols),
        (counts_hbm, counts),
        (item_hbm, item),
        (user_hbm, user),
        (masks_hbm.at[0], words.at[:, pl.ds(0, slot_total), :]),
        (vals_hbm.at[0], vals.at[pl.ds(0, slot_total)]),
    ]
    copies = [pltpu.make_async_copy(a, b, sems.at[i]) for i, (a, b) in enumerate(sources)]
    for copy in copies:
        copy.start()
    for copy in copies[:3]:
        copy.wait()
    invert_slots(lambda q: rows[0, q] * 4 + cols[0, q], counts[0], slots, 32, slot_total, slot_total)
    zero_spare(words, slot_total)
    patterns = bit_patterns()
    copies[3].wait()
    for j in range(4):
        right[tile(j), :] = item[pl.ds(pl.multiple_of(column_of(core, j) * T, T), T), :].astype(bf16)
    copies[4].wait()
    user_low = user[...].astype(bf16)
    predict = matmul(user_low[: 2 * T, :], right[...], 1, 1)
    copies[5].wait()
    copies[6].wait()
    for r in range(8):
        if r and r % 2 == 0:
            predict = matmul(user_low[r * T : (r + 2) * T, :], right[...], 1, 1)
        for j in range(4):
            slot = slots[r * 4 + column_of(core, j)]
            out = own_resid if j < 2 else other_resid
            for k2 in range(T // 16):
                part = slice(16 * k2, 16 * k2 + 16)
                seen = observed(patterns, words, slot, k2)
                diff = vals[slot, part, :].astype(f32) - predict[r % 2 * T + 16 * k2 : r % 2 * T + 16 * k2 + 16, tile(j)]
                out[j % 2, r * T + 16 * k2 : r * T + 16 * k2 + 16, :] = jnp.where(seen, diff, 0.0).astype(bf16)
    own_sum[...] = matmul(user_low, side(own_resid), 0, 0)
    other_sum[...] = matmul(user_low, side(other_resid), 0, 0)


def chip_sum(own_sum, arrived, kept, sent):
    total = own_sum[...] + arrived[...]
    kept[...] = total
    sent[...] = total.astype(bf16)


def cast_friends(friend, friend_low):
    friend_low[...] = friend[...].astype(bf16)


def eye_mask():
    return lax.broadcasted_iota(jnp.int32, (T, T), 0) == lax.broadcasted_iota(jnp.int32, (T, T), 1)


def update_rows(eye, factor, acc_row, prod):
    grad = shrinkage * factor - prod
    spread = jnp.where(eye, jnp.broadcast_to(acc_row, (T, T)), 0.0)
    acc = jnp.sum(grad * grad * (1.0 / T) + spread, axis=1, keepdims=True)
    new = factor - grad * (learn_rate * lax.rsqrt(acc))
    acc_out = jnp.sum(jnp.where(eye, jnp.broadcast_to(acc, (T, T)), 0.0), axis=0, keepdims=True)
    return new, acc_out


def first_users(own_resid, other_resid, user, item, acc, user_mid, acc_mid, user_low):
    core = lax.axis_index("grp") % 2
    eye = eye_mask()
    halves = []
    for first in (0, 2):
        parts = [item[pl.ds(pl.multiple_of(column_of(core, j) * T, T), T), :] for j in (first, first + 1)]
        halves.append(jnp.concatenate(parts, axis=0).astype(bf16))
    prod = matmul(side(own_resid), halves[0], 1, 0) + matmul(side(other_resid), halves[1], 1, 0)
    for r in range(8):
        new, acc_out = update_rows(eye, user[tile(r), :], acc[r : r + 1, :], prod[tile(r), :])
        user_mid[tile(r), :] = new
        user_low[tile(r), :] = new.astype(bf16)
        acc_mid[r : r + 1, :] = acc_out


def place_tiles(
    rows_hbm, cols_hbm, counts_hbm, trust_rows_hbm, trust_cols_hbm, trust_count,
    vals_hbm, masks_hbm, trust_hbm, trust_masks_hbm,
    placed, trust_placed, rows, cols, counts, trust_rows, trust_cols, vals, words, trust_vals, trust_words, slots, sems,
):
    core = lax.axis_index("grp") % 2
    rate_total, trust_total = vals_hbm.shape[1], trust_hbm.shape[0]
    sources = [
        (vals_hbm.at[1], vals.at[pl.ds(0, rate_total)]),
        (masks_hbm.at[1], words.at[:, pl.ds(0, rate_total), :]),
        (trust_hbm, trust_vals.at[pl.ds(0, trust_total)]),
        (trust_masks_hbm, trust_words.at[:, pl.ds(0, trust_total), :]),
        (rows_hbm, rows),
        (cols_hbm, cols),
        (counts_hbm, counts),
        (trust_rows_hbm, trust_rows),
        (trust_cols_hbm, trust_cols),
    ]
    copies = [pltpu.make_async_copy(a, b, sems.at[i]) for i, (a, b) in enumerate(sources)]
    for copy in copies[4:] + copies[:4]:
        copy.start()
    for copy in copies[4:]:
        copy.wait()
    zero_spare(words, rate_total)
    zero_spare(trust_words, trust_total)
    patterns = bit_patterns()
    invert_slots(lambda q: rows[1, q] * 4 + cols[1, q], counts[1], slots, 32, rate_total, rate_total)
    copies[0].wait()
    copies[1].wait()

    def place(slot, values, packed, out, r, c):
        for k2 in range(T // 16):
            seen = observed(patterns, packed, slot, k2)
            value = jnp.where(seen, values[slot, 16 * k2 : 16 * k2 + 16, :].astype(f32), UNSEEN)
            out[c, pl.ds(pl.multiple_of(r * T + 16 * k2, 16), 16), :] = value

    @pl.loop(0, 8)
    def _(r):
        for j in range(4):
            place(slots[r * 4 + column_of(core, j)], vals, words, placed, r, j)

    invert_slots(lambda q: trust_rows[q] * 8 + trust_cols[q], trust_count[0], slots, 64, trust_total, trust_total)
    copies[2].wait()
    copies[3].wait()

    @pl.loop(0, 8)
    def _(r):
        for c in range(8):
            place(slots[r * 8 + c], trust_vals, trust_words, trust_placed, r, c)


def update_items(kept, arrived, item, acc, share, item_low):
    core = lax.axis_index("grp") % 2
    near = lax.axis_index("grp") // 2
    eye = eye_mask()
    total = kept[...] + arrived[...].astype(f32)
    share[T : T + 8, :] = jnp.zeros((8, T), f32)
    for j in range(2):
        column = column_of(core, j)
        factor = item[pl.ds(pl.multiple_of(column * T, T), T), :]
        new, acc_out = update_rows(eye, factor, acc[pl.ds(column, 1), :], total[:, tile(j)].T)
        item_low[tile(j), :] = new.astype(bf16)

        @pl.when(near == j)
        def _():
            share[:T, :] = new
            share[T : T + 1, :] = acc_out


def side(resid):
    return jnp.concatenate([resid[j] for j in range(resid.shape[0])], axis=1)


def residuals(left, right, placed, column, out, height=8):
    count = right.shape[0] // T
    for r in range(8 // height):
        part = slice(r * height * T, (r + 1) * height * T)
        predict = matmul(left[part, :], right[...], 1, 1)
        for j in range(count):
            value = placed[column + j, part, :]
            out[j, part, :] = jnp.where(value < SEEN_BELOW, value - predict[:, tile(j)], 0.0).astype(bf16)


def own_columns(user_low, own_low, placed, own_resid, own_sum, own_prod):
    residuals(user_low, own_low, placed, 0, own_resid, 2)
    resid = side(own_resid)
    own_sum[...] = matmul(user_low[...], resid, 0, 0)
    own_prod[...] = matmul(resid, own_low[...], 1, 0)


def second_stratum(
    user_low, other_low, placed, own_prod, user_mid, acc_mid, far_low, trust_placed,
    other_resid, user_rated, acc_rated, rated_low, trust_resid, friend_sum,
):
    eye = eye_mask()
    residuals(user_low, other_low, placed, 2, other_resid)
    prod = own_prod[...] + matmul(side(other_resid), other_low[...], 1, 0)
    for r in range(8):
        new, acc_out = update_rows(eye, user_mid[tile(r), :], acc_mid[r : r + 1, :], prod[tile(r), :])
        user_rated[tile(r), :] = new
        rated_low[tile(r), :] = new.astype(bf16)
        acc_rated[r : r + 1, :] = acc_out
    residuals(rated_low, far_low.at[pl.ds(0, 4 * T)], trust_placed, 0, trust_resid)
    friend_sum[...] = matmul(rated_low[...], side(trust_resid), 0, 0).astype(bf16)


def second_half(rated_low, far_low, trust_placed, trust_resid, friend_sum):
    residuals(rated_low, far_low.at[pl.ds(4 * T, 4 * T)], trust_placed, 4, trust_resid)
    friend_sum[...] = matmul(rated_low[...], side(trust_resid), 0, 0).astype(bf16)


def item_products(user_low, other_resid, other_sum):
    other_sum[...] = matmul(user_low[...], side(other_resid), 0, 0)


def split_sum(own_sum, arrived, kept, sent):
    flip = lax.axis_index("grp") // 2 == 1
    total = own_sum[...] + arrived[...]
    kept[...] = jnp.where(flip, total[:, T:], total[:, :T])
    sent[...] = jnp.where(flip, total[:, :T], total[:, T:])


def last_users(first_resid, second_resid, far_low, user_rated, acc_rated, user_out, acc_out):
    eye = eye_mask()
    half = 4 * T
    prod = matmul(side(first_resid), far_low[:half, :], 1, 0) + matmul(side(second_resid), far_low[half:, :], 1, 0)
    for r in range(8):
        new, acc = update_rows(eye, user_rated[tile(r), :], acc_rated[r : r + 1, :], prod[tile(r), :])
        user_out[tile(r), :] = new
        acc_out[r : r + 1, :] = acc


def friend_rows(eye, home, friend, acc, first, rows, acc_rows):
    for j in range(4):
        r = first + j
        new, acc_row = update_rows(eye, friend[tile(r), :], acc[r : r + 1, :], home[:, tile(j)].astype(f32).T)
        rows[tile(j), :] = new
        acc_rows[r : r + 1, :] = acc_row


def move_out(pairs, sems):
    copies = [pltpu.make_async_copy(a, b, sems.at[i]) for i, (a, b) in enumerate(pairs)]
    for copy in copies:
        copy.start()
    for copy in copies:
        copy.wait()


def first_friends(
    home, friend, acc, kept, arrived, share,
    friend_out, item_out, item_acc_out, acc_rows,
    rows, item_rows, item_acc, sems,
):
    eye = eye_mask()
    new, acc_row = update_rows(eye, share[:T, :], share[T : T + 1, :], (kept[...] + arrived[...]).T)
    item_rows[...] = new
    item_acc[...] = acc_row
    acc_rows[4:8, :] = acc[4:8, :]
    friend_rows(eye, home, friend, acc, 0, rows, acc_rows)
    move_out([(rows, friend_out.at[pl.ds(0, 4 * T)]), (item_rows, item_out), (item_acc, item_acc_out)], sems)


def other_friends(home, friend, acc, earlier, friend_out, acc_out, rows, acc_rows, sems):
    del earlier
    acc_rows[0:4, :] = acc[0:4, :]
    friend_rows(eye_mask(), home, friend, acc, 4, rows, acc_rows)
    move_out([(rows, friend_out.at[pl.ds(4 * T, 4 * T)]), (acc_rows, acc_out)], sems)


def local(
    user_factors, user_accum, friend_factors, friend_accum, item_factors, item_accum,
    rating_values, rating_masks, rating_rows, rating_cols, rating_counts,
    trust_values, trust_masks, trust_rows, trust_cols, trust_counts,
):
    blocks, groups = lax.axis_size("blk"), lax.axis_size("grp")
    axes = ("blk", "grp")

    def send(value, to):
        route = []
        for b in range(blocks):
            for g in range(groups):
                tb, tg = to(b, g)
                route.append((b * groups + g, tb % blocks * groups + tg))
        return lax.ppermute(value, axes, route)

    words_of = rating_masks.transpose(0, 2, 1, 3)
    trust_words_of = trust_masks.transpose(1, 0, 2)
    user_acc = user_accum.reshape(8, T)
    friend_acc = friend_accum.reshape(8, T)
    item_acc = item_accum.reshape(4, T)
    counts = rating_counts.reshape(2)

    own_sum, other_sum, own_resid, other_resid = call(
        first_stratum,
        [HBM] * 7,
        [shape((T, 2 * T), f32), shape((T, 2 * T), f32), shape((2, 8 * T, T), bf16), shape((2, 8 * T, T), bf16)],
        [
            pltpu.SMEM((2, 32), jnp.int32), pltpu.SMEM((2, 32), jnp.int32), pltpu.SMEM((2,), jnp.int32),
            pltpu.VMEM((8 * T, T), f32), pltpu.VMEM((4 * T, T), f32),
            pltpu.VMEM((33, T, T), bf16), pltpu.VMEM((10, 40, T), jnp.int32), pltpu.SMEM((40,), jnp.int32),
            pltpu.VMEM((4 * T, T), bf16), pltpu.SemaphoreType.DMA((7,)),
        ],
        270_000_000, 3_000_000,
    )(rating_rows, rating_cols, counts, user_factors, item_factors, rating_values, words_of)

    arrived = send(other_sum, lambda b, g: (b, g ^ 1))
    half_bit = blocks // 2
    friend_low = call(cast_friends, [VM], [shape((8 * T, T), bf16)], [], 100_000, 800_000)(friend_factors)[0]
    far_low = send(friend_low, lambda b, g: (b ^ half_bit, g))
    kept, sent = call(
        chip_sum, [VM, VM], [shape((T, 2 * T), f32), shape((T, 2 * T), bf16)], [], 100_000, 300_000
    )(own_sum, arrived)
    arrived = send(sent, lambda b, g: (b, g ^ 2))
    share, own_low = call(
        update_items,
        [VM] * 4,
        [shape((T + 8, T), f32), shape((2 * T, T), bf16)],
        [], 1_000_000, 500_000,
    )(kept, arrived, item_factors, item_acc)
    own_low = send(own_low, lambda b, g: (b + 1, g))
    share = send(share, lambda b, g: (b + 1, g))
    user_mid, acc_mid, user_low = call(
        first_users,
        [VM] * 5,
        [shape((8 * T, T), f32), shape((8, T), f32), shape((8 * T, T), bf16)],
        [], 140_000_000, 3_000_000,
    )(own_resid, other_resid, user_factors, item_factors, user_acc)
    placed, trust_placed = call(
        place_tiles,
        [HBM] * 5 + [SM] + [HBM] * 4,
        [shape((4, 8 * T, T), f32), shape((8, 8 * T, T), f32)],
        [
            pltpu.SMEM((2, 32), jnp.int32), pltpu.SMEM((2, 32), jnp.int32), pltpu.SMEM((2,), jnp.int32),
            pltpu.SMEM((48,), jnp.int32), pltpu.SMEM((48,), jnp.int32),
            pltpu.VMEM((33, T, T), bf16), pltpu.VMEM((10, 40, T), jnp.int32),
            pltpu.VMEM((49, T, T), bf16), pltpu.VMEM((10, 56, T), jnp.int32),
            pltpu.SMEM((72,), jnp.int32), pltpu.SemaphoreType.DMA((9,)),
        ],
        20_000_000, 6_000_000,
    )(rating_rows, rating_cols, counts, trust_rows, trust_cols, trust_counts, rating_values, words_of, trust_values, trust_words_of)

    other_low = send(own_low, lambda b, g: (b, g ^ 1))
    _, own_sum, own_prod = call(
        own_columns,
        [VM] * 3,
        [shape((2, 8 * T, T), bf16), shape((T, 2 * T), f32), shape((8 * T, T), f32)],
        [], 200_000_000, 1_500_000,
    )(user_low, own_low, placed)
    other_resid, user_rated, acc_rated, rated_low, trust_a, friend_a = call(
        second_stratum,
        [VM] * 8,
        [
            shape((2, 8 * T, T), bf16), shape((8 * T, T), f32), shape((8, T), f32), shape((8 * T, T), bf16),
            shape((4, 8 * T, T), bf16), shape((T, 4 * T), bf16),
        ],
        [], 400_000_000, 6_000_000,
    )(user_low, other_low, placed, own_prod, user_mid, acc_mid, far_low, trust_placed)
    home_a = send(friend_a, lambda b, g: (b ^ half_bit, g))
    trust_b, friend_b = call(
        second_half,
        [VM] * 3,
        [shape((4, 8 * T, T), bf16), shape((T, 4 * T), bf16)],
        [], 270_000_000, 3_000_000,
    )(rated_low, far_low, trust_placed)
    home_b = send(friend_b, lambda b, g: (b ^ half_bit, g))
    other_sum = call(
        item_products, [VM] * 2, [shape((T, 2 * T), f32)], [], 70_000_000, 900_000
    )(user_low, other_resid)[0]
    arrived = send(other_sum, lambda b, g: (b, g ^ 1))
    user_out, user_acc_out = call(
        last_users,
        [VM] * 5,
        [shape((8 * T, T), f32), shape((8, T), f32)],
        [], 270_000_000, 4_000_000,
    )(trust_a, trust_b, far_low, user_rated, acc_rated)
    kept, sent = call(split_sum, [VM, VM], [shape((T, T), f32)] * 2, [], 100_000, 400_000)(own_sum, arrived)
    arrived = send(sent, lambda b, g: (b, g ^ 2))
    friend_out, item_out, item_acc_out, friend_acc_mid = call(
        first_friends,
        [VM] * 6,
        [shape((8 * T, T), f32), shape((T, T), f32), shape((1, T), f32), shape((8, T), f32)],
        [pltpu.VMEM((4 * T, T), f32), pltpu.VMEM((T, T), f32), pltpu.VMEM((1, T), f32), pltpu.SemaphoreType.DMA((3,))],
        3_000_000, 1_200_000, out_specs=[HBM, HBM, HBM, VM],
    )(home_a, friend_factors, friend_acc, kept, arrived, share)
    friend_out, friend_acc_out = call(
        other_friends,
        [VM] * 3 + [HBM],
        [shape((8 * T, T), f32), shape((8, T), f32)],
        [pltpu.VMEM((4 * T, T), f32), pltpu.VMEM((8, T), f32), pltpu.SemaphoreType.DMA((2,))],
        2_000_000, 900_000, out_specs=[HBM] * 2, aliases={3: 0},
    )(home_b, friend_factors, friend_acc_mid, friend_out)
    return (
        user_out,
        user_acc_out.reshape(8 * T),
        friend_out,
        friend_acc_out.reshape(8 * T),
        item_out,
        item_acc_out.reshape(T),
    )


def solution(mesh):
    both = ("blk", "grp")
    return jax.shard_map(
        local,
        mesh=mesh,
        in_specs=(
            P(both, None), P(both), P(both, None), P(both), P("blk", None), P("blk"),
            P(None, both, None, None), P(None, both, None, None), P(None, both), P(None, both), P(None, both),
            P(both, None, None), P(both, None, None), P(both), P(both), P(both),
        ),
        out_specs=(P(both, None), P(both), P(both, None), P(both), P(both, None), P(both)),
        check_vma=False,
    )
```
